32 devices in a mesh: groups: 2 (over y), wide: 8 (over z, x), short: 2 (over core).
Axes of the slice: x: 2, y: 2, z: 4, core: 2. Of those that a mesh axis runs over, the one named last changes fastest.
Arguments:
- tokens: bfloat16 [64, 5120], P(('groups', 'wide'), 'short'), parts along dimension 0, may hold values from -6 to 6
- norm_gain: float32 [5120], P('short'), may hold values from 0.5 to 1.5
- mixer_in: bfloat16 [5120, 2, 5888], P('short', None, 'wide'), may hold values from -0.078125 to 0.078125
- shared_in: bfloat16 [5120, 512], P('short', 'wide'), may hold values from -0.078125 to 0.078125
- step_in: bfloat16 [5120, 32], P('short'), may hold values from -0.078125 to 0.078125
- step_bias: float32 [32], P('short'), may hold values from -2 to 1
- decay_rate: float32 [32], P('short'), may hold values from 0.05 to 4
- skip_gain: float32 [32], P('short'), may hold values from 0.2 to 1.5
- cached_keys: bfloat16 [16, 512, 512], P(('groups', 'wide'), None, 'short'), parts along dimension 0, may hold values from -64 to 64
- cached_values: bfloat16 [16, 512, 512], P(('groups', 'wide'), None, 'short'), parts along dimension 0, may hold values from -6 to 6
- lengths: int32 [16], P(('groups', 'wide')), parts along dimension 0, may hold values from 2 to 512, as said below
- state_cache: bfloat16 [16, 32, 128, 256], P(('groups', 'wide'), 'short'), parts along dimension 0, may hold values from -6 to 6
- mixer_gain: float32 [4096], P('short'), may hold values from 0.5 to 1.5
- mixer_out: bfloat16 [2, 3328, 5120], P(None, 'wide', 'short'), may hold values from -0.078125 to 0.078125
- gate_weight: bfloat16 [5120, 21504], P('short', 'wide'), may hold values from -0.078125 to 0.078125
- up_weight: bfloat16 [5120, 21504], P('short', 'wide'), may hold values from -0.078125 to 0.078125
- down_weight: bfloat16 [21504, 5120], P('wide', 'short'), may hold values from -0.0390625 to 0.0390625
Outputs:
- mixed: bfloat16 [64, 5120], P(('groups', 'wide'), 'short'), parts along dimension 0
The draws below stay inside these ranges and needn't reach their ends.
There are 2 independent parts, one for each index of `groups`. The reference program is written for one: setup_inputs(seed, part) draws one part's arguments, and reference() takes and returns one part's arrays. A program takes and returns all parts, laid end to end along the dimension named above; an argument that names none is the same for every part. Nothing has to cross between parts.
Inputs may be any that keep to these rules, and one draw needn't show every extreme that they name: `lengths`: in every draw some request holds exactly 512 earlier tokens.
All inputs are finite; a program needn't handle non-finite values.
Results may differ from the reference program's by a relative error of at most 0.009.
Values may be sent and summed in bfloat16 or wider, within the bound.
A program may use at most 128 MiB of HBM per device.

```python
import math
import jax
import jax.numpy as jnp
from jax import lax

D = 5120
QUERY_HEADS = 20
KEY_VALUE_HEADS = 4
HEAD_SIZE = 128
MH = 32
MP = 128
NS = 256
FF = 21504
CACHE_SLOTS = 512
DRAFT_TOKENS = 4
HEAD_GROUPS = 2
REQUEST_COUNT = 8
ROWS = 32
GCOL = 5888
OCOL = 3328


def draw_lengths(key, part):
    drawn = jax.random.randint(key, (REQUEST_COUNT,), 2, CACHE_SLOTS + 1)
    chosen = jax.random.randint(jax.random.fold_in(key, 11), (), 0, REQUEST_COUNT)
    return jnp.where(jnp.arange(REQUEST_COUNT) == chosen, CACHE_SLOTS, drawn).astype(jnp.int32)


def draw_cached_keys(key, part):
    cache_entries = jax.random.normal(key, (REQUEST_COUNT, CACHE_SLOTS, KEY_VALUE_HEADS * HEAD_SIZE), jnp.float32)
    return jnp.clip(cache_entries, -64.0, 64.0).astype(jnp.bfloat16)


def block_levels(key, extent, shards, smallest, top_value):
    def one(axis_at, blocks):
        draws = jax.random.uniform(jax.random.fold_in(jax.random.fold_in(key, 6), axis_at), (blocks,), jnp.float32, smallest / len(shards), top_value / len(shards))
        return jnp.repeat(jnp.exp(draws), extent[axis_at] // blocks).reshape((-1,) + (1,) * (len(extent) - axis_at - 1))

    level = one(*shards[0])
    for cut in shards[1:]:
        level = level * one(*cut)
    return level


def normal_values(key, shape, spread, bound, cuts=(), kind=jnp.bfloat16):
    result = jax.random.normal(key, shape, jnp.float32) * spread
    if len(cuts) > 0:
        result = block_levels(key, shape, cuts, -0.22, 0.18) * result
    return jnp.clip(result, min=-bound, max=bound).astype(kind)


def setup_inputs(seed: int = 0, part: int = 0) -> dict:
    key_list = jax.random.split(jax.random.key(seed), 18)
    part_splits = jax.random.split(jax.random.fold_in(key_list[17], part), 18)
    return {
        "tokens": normal_values(part_splits[0], (ROWS, D), 1.0, 6.0, ((0, 8), (1, 2))),
        "norm_gain": jnp.clip(1.0 + 0.1 * jax.random.normal(key_list[1], (D,), jnp.float32), 0.5, 1.5),
        "mixer_in": normal_values(key_list[2], (D, HEAD_GROUPS, GCOL), D ** -0.5, 0.078125, ((0, 2), (2, 8))),
        "shared_in": normal_values(key_list[3], (D, 2 * NS), D ** -0.5, 0.078125, ((0, 2), (1, 8))),
        "step_in": normal_values(key_list[4], (D, MH), D ** -0.5, 0.078125, ((0, 2),)),
        "step_bias": jnp.clip(-2.0 + 3.0 * jax.random.uniform(key_list[5], (MH,), jnp.float32) ** block_levels(key_list[5], (MH,), ((0, 2),), -0.2, 0.2), -2.0, 1.0),
        "decay_rate": jnp.clip(jnp.exp(math.log(4.0) - 4.3820266 * jax.random.uniform(key_list[6], (MH,), jnp.float32) ** block_levels(key_list[6], (MH,), ((0, 2),), -0.2, 0.2)), 0.05, 4.0),
        "skip_gain": jnp.clip(0.2 + 1.3 * jax.random.uniform(key_list[7], (MH,), jnp.float32) ** block_levels(key_list[7], (MH,), ((0, 2),), -0.2, 0.2), 0.2, 1.5),
        "cached_keys": draw_cached_keys(jax.random.fold_in(jax.random.fold_in(key_list[17], part), 71), part),
        "cached_values": normal_values(part_splits[9], (REQUEST_COUNT, CACHE_SLOTS, KEY_VALUE_HEADS * HEAD_SIZE), 1.0, 6.0, ((0, 8), (2, 2))),
        "lengths": draw_lengths(jax.random.fold_in(jax.random.fold_in(key_list[17], part), 71), part),
        "state_cache": normal_values(part_splits[11], (REQUEST_COUNT, MH, MP, NS), 1.0, 6.0, ((0, 8), (1, 2))),
        "mixer_gain": jnp.clip(1.0 + 0.1 * jax.random.normal(key_list[12], (MH * MP,), jnp.float32), 0.5, 1.5),
        "mixer_out": normal_values(key_list[13], (HEAD_GROUPS, OCOL, D), (HEAD_GROUPS * OCOL) ** -0.5, 0.078125, ((1, 8), (2, 2))),
        "gate_weight": normal_values(key_list[14], (D, FF), D ** -0.5, 0.078125, ((0, 2), (1, 8))),
        "up_weight": normal_values(key_list[15], (D, FF), D ** -0.5, 0.078125, ((0, 2), (1, 8))),
        "down_weight": normal_values(key_list[16], (FF, D), FF ** -0.5, 0.0390625, ((0, 8), (1, 2))),
    }


epsilon = 1e-05

def rotate(vectors, cos_table, sin_table):
    half_width = vectors.shape[-1] // 2
    first_half = vectors[..., :half_width]
    second_half = vectors[..., half_width:]
    return jnp.concatenate([first_half * cos_table - second_half * sin_table, second_half * cos_table + first_half * sin_table], axis=-1)

def rope_tables(positions):
    frequency = 10000.0 ** (-(jnp.arange(HEAD_SIZE // 2, dtype=jnp.float32) * 2.0 / HEAD_SIZE))
    angles = positions.astype(jnp.float32)[..., None] * frequency
    return (jnp.cos(angles), jnp.sin(angles))

def attend_one(packed):
    queries, fresh_keys, fresh_values, key_tile_block, value_tile_block, length = packed
    score_scale = HEAD_SIZE ** (-0.5)
    query_float = queries.astype(jnp.float32)
    scores_cache = jnp.einsum('tkgd,pkd->kgtp', query_float, key_tile_block.astype(jnp.float32)) * score_scale
    scores_new = jnp.einsum('tkgd,ukd->kgtu', query_float, fresh_keys.astype(jnp.float32)) * score_scale
    live_keys = jnp.arange(key_tile_block.shape[0], dtype=jnp.int32) < length
    causal = jnp.arange(DRAFT_TOKENS)[None, :] <= jnp.arange(DRAFT_TOKENS)[:, None]
    scores_cache = jnp.where(live_keys, scores_cache, -1e+30)
    scores_new = jnp.where(causal, scores_new, -1e+30)
    highest = jnp.maximum(lax.optimization_barrier(jnp.max(scores_cache, axis=-1)), lax.optimization_barrier(jnp.max(scores_new, axis=-1)))[..., None]
    weight_cache = jnp.exp(scores_cache - highest)
    weight_new = jnp.exp(scores_new - highest)
    denominator = lax.optimization_barrier(jnp.sum(weight_cache, axis=-1, keepdims=True)) + lax.optimization_barrier(jnp.sum(weight_new, axis=-1, keepdims=True))
    probs_cache = (weight_cache / denominator).astype(jnp.bfloat16)
    probs_new = (weight_new / denominator).astype(jnp.bfloat16)
    attended = jnp.einsum('kgtp,pkd->tkgd', probs_cache.astype(jnp.float32), value_tile_block.astype(jnp.float32))
    attended = attended + jnp.einsum('kgtu,ukd->tkgd', probs_new.astype(jnp.float32), fresh_values.astype(jnp.float32))
    return attended.astype(jnp.bfloat16)

def scan_one(state_block, inputs_x, gates_z, b_vals, c_vals, step_sizes, decay_rates, skip_gain, head_gain):
    hstate = state_block.astype(jnp.float32)
    in_active = jax.nn.silu(inputs_x.astype(jnp.float32))
    write_vec = jax.nn.silu(b_vals.astype(jnp.float32))
    read_vec = jax.nn.silu(c_vals.astype(jnp.float32))
    outputs = []
    for draft_index in range(DRAFT_TOKENS):
        decays = jnp.exp(-step_sizes[draft_index] * decay_rates)
        inject = (step_sizes[draft_index][:, None] * in_active[draft_index])[:, :, None] * write_vec[draft_index][None, None, :]
        hstate = decays[:, None, None] * hstate + inject
        readout = jnp.einsum('hpn,n->hp', hstate, read_vec[draft_index], precision=lax.Precision.HIGHEST)
        outputs.append(readout + skip_gain[:, None] * in_active[draft_index])
    gated = jnp.stack(outputs) * jax.nn.silu(gates_z.astype(jnp.float32))
    mean_square = lax.optimization_barrier(jnp.mean(gated * gated, axis=-1, keepdims=True))
    return (gated * lax.rsqrt(mean_square + epsilon) * head_gain).astype(jnp.bfloat16)

def reference(tokens, norm_gain, mixer_in, shared_in, step_in, step_bias, decay_rate, skip_gain, cached_keys, cached_values, lengths, state_cache, mixer_gain, mixer_out, gate_weight, up_weight, down_weight):
    q_heads = QUERY_HEADS // HEAD_GROUPS
    key_value_heads = KEY_VALUE_HEADS // HEAD_GROUPS
    ssm_heads = MH // HEAD_GROUPS
    repeat_factor = QUERY_HEADS // KEY_VALUE_HEADS
    query_size = q_heads * HEAD_SIZE
    key_size = key_value_heads * HEAD_SIZE
    m_size = ssm_heads * MP
    rows_float = tokens.astype(jnp.float32)
    inv_rms = lax.rsqrt(lax.optimization_barrier(jnp.mean(rows_float * rows_float, axis=1, keepdims=True)) + epsilon)
    normed = (rows_float * inv_rms * norm_gain[None, :]).astype(jnp.bfloat16)
    grouped_heads = jnp.dot(normed, mixer_in.reshape(D, HEAD_GROUPS * GCOL), preferred_element_type=jnp.float32).astype(jnp.bfloat16)
    grouped_heads = grouped_heads.reshape(ROWS, HEAD_GROUPS, GCOL)
    shared = jnp.dot(normed, shared_in, preferred_element_type=jnp.float32).astype(jnp.bfloat16)
    step_raw = jnp.dot(normed, step_in, preferred_element_type=jnp.float32)
    gate_sum = jnp.dot(normed, gate_weight, preferred_element_type=jnp.float32)
    up_sum = jnp.dot(normed, up_weight, preferred_element_type=jnp.float32)
    hidden = (jax.nn.silu(gate_sum) * up_sum).astype(jnp.bfloat16)
    queries = grouped_heads[:, :, :query_size].reshape(REQUEST_COUNT, DRAFT_TOKENS, QUERY_HEADS, HEAD_SIZE)
    fresh_keys = grouped_heads[:, :, query_size:query_size + key_size].reshape(REQUEST_COUNT, DRAFT_TOKENS, KEY_VALUE_HEADS, HEAD_SIZE)
    fresh_values = grouped_heads[:, :, query_size + key_size:query_size + 2 * key_size].reshape(REQUEST_COUNT, DRAFT_TOKENS, KEY_VALUE_HEADS, HEAD_SIZE)
    x_start = query_size + 2 * key_size
    inputs_x = grouped_heads[:, :, x_start:x_start + m_size].reshape(REQUEST_COUNT, DRAFT_TOKENS, MH, MP)
    gates_z = grouped_heads[:, :, x_start + m_size:x_start + 2 * m_size].reshape(REQUEST_COUNT, DRAFT_TOKENS, MH, MP)
    positions = lengths[:, None] + jnp.arange(DRAFT_TOKENS, dtype=jnp.int32)[None, :]
    cos_table, sin_table = rope_tables(positions)
    cos_table = cos_table[:, :, None, :]
    sin_table = sin_table[:, :, None, :]
    rotated_queries = rotate(queries.astype(jnp.float32), cos_table, sin_table).astype(jnp.bfloat16)
    keys_rot = rotate(fresh_keys.astype(jnp.float32), cos_table, sin_table).astype(jnp.bfloat16)
    rotated_queries = rotated_queries.reshape(REQUEST_COUNT, DRAFT_TOKENS, KEY_VALUE_HEADS, repeat_factor, HEAD_SIZE)
    key_tile_block = cached_keys.reshape(REQUEST_COUNT, CACHE_SLOTS, KEY_VALUE_HEADS, HEAD_SIZE)
    value_tile_block = cached_values.reshape(REQUEST_COUNT, CACHE_SLOTS, KEY_VALUE_HEADS, HEAD_SIZE)
    attention = lax.map(attend_one, (rotated_queries, keys_rot, fresh_values, key_tile_block, value_tile_block, lengths))
    step_sizes = jax.nn.softplus(step_raw.reshape(REQUEST_COUNT, DRAFT_TOKENS, MH) + step_bias[None, None, :])
    b_vals = shared[:, :NS].reshape(REQUEST_COUNT, DRAFT_TOKENS, NS)
    c_vals = shared[:, NS:].reshape(REQUEST_COUNT, DRAFT_TOKENS, NS)
    head_gain = mixer_gain.reshape(MH, MP)

    def mamba_one(packed):
        return scan_one(packed[0], packed[1], packed[2], packed[3], packed[4], packed[5], decay_rate, skip_gain, head_gain)
    mamba = lax.map(mamba_one, (state_cache, inputs_x, gates_z, b_vals, c_vals, step_sizes))
    mixer_rows = jnp.concatenate([attention.reshape(ROWS, HEAD_GROUPS, query_size), mamba.reshape(ROWS, HEAD_GROUPS, m_size)], axis=2)
    summed = jnp.dot(mixer_rows.reshape(ROWS, HEAD_GROUPS * OCOL), mixer_out.reshape(HEAD_GROUPS * OCOL, D), preferred_element_type=jnp.float32)
    summed = summed + jnp.dot(hidden, down_weight, preferred_element_type=jnp.float32)
    return (rows_float + summed).astype(jnp.bfloat16)
```

```python
import functools
import math
import jax
import jax.numpy as jnp
from jax import lax
from jax.experimental import pallas as pl
from jax.experimental.pallas import tpu as pltpu
from jax.sharding import PartitionSpec as P

D = 5120
QUERY_HEADS = 20
KEY_VALUE_HEADS = 4
HEAD_SIZE = 128
MH = 32
MP = 128
NS = 256
CACHE_SLOTS = 512
DRAFT_TOKENS = 4


epsilon = 1e-05


def as_sent(x):

    def short(part):
        return part.astype(jnp.bfloat16) if part.dtype == jnp.float32 else part

    return jax.tree.map(short, x)


def rotate(vectors, cos_table, sin_table):
    half_width = vectors.shape[-1] // 2
    first_half = vectors[..., :half_width]
    second_half = vectors[..., half_width:]
    return jnp.concatenate(
        [
            first_half * cos_table - second_half * sin_table,
            second_half * cos_table + first_half * sin_table,
        ],
        axis=-1,
    )


def rope_tables(positions):
    frequency = 10000.0 ** (-(jnp.arange(HEAD_SIZE // 2, dtype=jnp.float32) * 2.0 / HEAD_SIZE))
    angles = positions.astype(jnp.float32)[..., None] * frequency
    return (jnp.cos(angles), jnp.sin(angles))


def attend_one(queries, fresh_keys, fresh_values, key_tile_block, value_tile_block, length):
    score_scale = HEAD_SIZE ** (-0.5)
    scores_cache = (
        jnp.einsum("tkgd,pkd->kgtp", queries, key_tile_block, preferred_element_type=jnp.float32)
        * score_scale
    )
    scores_new = (
        jnp.einsum("tkgd,ukd->kgtu", queries, fresh_keys, preferred_element_type=jnp.float32)
        * score_scale
    )
    live_keys = jnp.arange(key_tile_block.shape[0], dtype=jnp.int32) < length
    causal = jnp.arange(DRAFT_TOKENS)[None, :] <= jnp.arange(DRAFT_TOKENS)[:, None]
    scores_cache = jnp.where(live_keys, scores_cache, -1e30)
    scores_new = jnp.where(causal, scores_new, -1e30)
    highest = jnp.maximum(jnp.max(scores_cache, axis=-1), jnp.max(scores_new, axis=-1))[..., None]
    weight_cache = jnp.exp(scores_cache - highest)
    weight_new = jnp.exp(scores_new - highest)
    denominator = jnp.sum(weight_cache, axis=-1, keepdims=True) + jnp.sum(
        weight_new, axis=-1, keepdims=True
    )
    probs_cache = (weight_cache / denominator).astype(jnp.bfloat16)
    probs_new = (weight_new / denominator).astype(jnp.bfloat16)
    attended = jnp.einsum(
        "kgtp,pkd->tkgd", probs_cache, value_tile_block, preferred_element_type=jnp.float32
    )
    attended = attended + jnp.einsum(
        "kgtu,ukd->tkgd", probs_new, fresh_values, preferred_element_type=jnp.float32
    )
    return attended.astype(jnp.bfloat16)


def scan_one(
    state_block, inputs_x, gates_z, b_vals, c_vals, step_sizes, decay_rates, skip_gain, head_gain
):
    hstate = state_block.astype(jnp.float32)
    in_active = jax.nn.silu(inputs_x.astype(jnp.float32))
    write_vec = jax.nn.silu(b_vals.astype(jnp.float32))
    read_vec = jax.nn.silu(c_vals.astype(jnp.float32))
    outputs = []
    for draft_index in range(DRAFT_TOKENS):
        decays = jnp.exp(-step_sizes[draft_index] * decay_rates)
        inject = (step_sizes[draft_index][:, None] * in_active[draft_index])[
            :, :, None
        ] * write_vec[draft_index][None, None, :]
        hstate = decays[:, None, None] * hstate + inject
        readout = jnp.einsum(
            "hpn,n->hp", hstate, read_vec[draft_index], precision=lax.Precision.HIGHEST
        )
        outputs.append(readout + skip_gain[:, None] * in_active[draft_index])
    gated = jnp.stack(outputs) * jax.nn.silu(gates_z.astype(jnp.float32))
    mean_square = jnp.mean(gated * gated, axis=-1, keepdims=True)
    return (gated * lax.rsqrt(mean_square + epsilon) * head_gain).astype(jnp.bfloat16)


def on_device(
    tokens,
    norm_gain,
    mixer_in,
    shared_in,
    step_in,
    step_bias,
    decay_rate,
    skip_gain,
    cached_keys,
    cached_values,
    lengths,
    state_cache,
    mixer_gain,
    mixer_out,
    gate_weight,
    up_weight,
    down_weight,
):
    short_count = lax.axis_size("short")
    n_wide = lax.axis_size("wide")
    q_heads = QUERY_HEADS // short_count
    key_value_heads = KEY_VALUE_HEADS // short_count
    ssm_heads = MH // short_count
    repeat_factor = QUERY_HEADS // KEY_VALUE_HEADS
    query_size = q_heads * HEAD_SIZE
    key_size = key_value_heads * HEAD_SIZE
    m_size = ssm_heads * MP
    local_rows = tokens.shape[0]
    requests = local_rows // DRAFT_TOKENS
    width_half = tokens.shape[1]
    rows_float = tokens.astype(jnp.float32)
    square_sum = lax.psum(jnp.sum(rows_float * rows_float, axis=1), "short")
    inv_rms = lax.rsqrt(square_sum / D + epsilon)
    normed = (rows_float * inv_rms[:, None] * norm_gain[None, :]).astype(jnp.bfloat16)
    step_terms = jnp.dot(normed, step_in, preferred_element_type=jnp.float32)
    step_raw = lax.psum_scatter(step_terms, "short", scatter_dimension=1, tiled=True)
    gathered = lax.all_gather(normed, "wide", axis=0, tiled=True)
    group_part = jnp.einsum("rd,dgc->rgc", gathered, mixer_in, preferred_element_type=jnp.float32)
    shared_part = jnp.dot(gathered, shared_in, preferred_element_type=jnp.float32)[:, None, :]
    gate_part = jnp.dot(gathered, gate_weight, preferred_element_type=jnp.float32)
    up_part = jnp.dot(gathered, up_weight, preferred_element_type=jnp.float32)
    gate_half, up_half = (
        lax.psum_scatter(
            gate_part.astype(jnp.bfloat16), "short", scatter_dimension=0, tiled=True
        ).astype(jnp.float32),
        lax.psum_scatter(
            up_part.astype(jnp.bfloat16), "short", scatter_dimension=0, tiled=True
        ).astype(jnp.float32),
    )
    hidden_half = (jax.nn.silu(gate_half) * up_half).astype(jnp.bfloat16)
    hidden = lax.all_gather(hidden_half, "short", axis=0, tiled=True)
    group_moved, shared_moved = (
        lax.all_to_all(group_part, "wide", split_axis=0, concat_axis=2, tiled=True),
        lax.all_to_all(shared_part, "wide", split_axis=0, concat_axis=2, tiled=True),
    )
    group_sum = lax.psum_scatter(group_moved, "short", scatter_dimension=1, tiled=True)
    shared_sum = lax.psum(shared_moved, "short")
    features = group_sum[:, 0, :].astype(jnp.bfloat16)
    shared_vals = shared_sum[:, 0, :].astype(jnp.bfloat16)
    queries = features[:, :query_size].reshape(requests, DRAFT_TOKENS, q_heads, HEAD_SIZE)
    fresh_keys = features[:, query_size : query_size + key_size].reshape(
        requests, DRAFT_TOKENS, key_value_heads, HEAD_SIZE
    )
    fresh_values = features[:, query_size + key_size : query_size + 2 * key_size].reshape(
        requests, DRAFT_TOKENS, key_value_heads, HEAD_SIZE
    )
    x_start = query_size + 2 * key_size
    inputs_x = features[:, x_start : x_start + m_size].reshape(
        requests, DRAFT_TOKENS, ssm_heads, MP
    )
    gates_z = features[:, x_start + m_size : x_start + 2 * m_size].reshape(
        requests, DRAFT_TOKENS, ssm_heads, MP
    )
    positions = lengths[:, None] + jnp.arange(DRAFT_TOKENS, dtype=jnp.int32)[None, :]
    cos_table, sin_table = rope_tables(positions)
    cos_table = cos_table[:, :, None, :]
    sin_table = sin_table[:, :, None, :]
    rotated_queries = rotate(queries.astype(jnp.float32), cos_table, sin_table).astype(jnp.bfloat16)
    keys_rot = rotate(fresh_keys.astype(jnp.float32), cos_table, sin_table).astype(jnp.bfloat16)
    rotated_queries = rotated_queries.reshape(
        requests, DRAFT_TOKENS, key_value_heads, repeat_factor, HEAD_SIZE
    )
    key_tile_block = cached_keys.reshape(requests, CACHE_SLOTS, key_value_heads, HEAD_SIZE)
    value_tile_block = cached_values.reshape(requests, CACHE_SLOTS, key_value_heads, HEAD_SIZE)
    attention = jax.vmap(attend_one)(
        rotated_queries, keys_rot, fresh_values, key_tile_block, value_tile_block, lengths
    )
    step_sizes = jax.nn.softplus(
        step_raw.reshape(requests, DRAFT_TOKENS, ssm_heads) + step_bias[None, None, :]
    )
    b_vals = shared_vals[:, :NS].reshape(requests, DRAFT_TOKENS, NS)
    c_vals = shared_vals[:, NS:].reshape(requests, DRAFT_TOKENS, NS)
    head_gain = mixer_gain.reshape(ssm_heads, MP)
    mamba = jax.vmap(scan_one, in_axes=(0, 0, 0, 0, 0, 0, None, None, None))(
        state_cache, inputs_x, gates_z, b_vals, c_vals, step_sizes, decay_rate, skip_gain, head_gain
    )
    own_rows = jnp.concatenate(
        [attention.reshape(local_rows, query_size), mamba.reshape(local_rows, m_size)], axis=1
    )
    returned = lax.all_to_all(
        as_sent(own_rows[:, None, :]), "wide", split_axis=2, concat_axis=0, tiled=True
    )
    both_groups = lax.all_gather(as_sent(returned), "short", axis=1, tiled=True).astype(
        returned.dtype
    )
    projected = jnp.einsum(
        "rgc,gcd->rd", both_groups, mixer_out, preferred_element_type=jnp.float32
    )
    summed = projected + jnp.dot(hidden, down_weight, preferred_element_type=jnp.float32)
    pieces = lax.all_to_all(
        summed.reshape(n_wide, local_rows, width_half).astype(jnp.bfloat16),
        "wide",
        split_axis=0,
        concat_axis=0,
        tiled=True,
    ).astype(jnp.float32)
    total = rows_float + jnp.sum(pieces, axis=0)
    return total.astype(jnp.bfloat16)


MESH = pl.DeviceIdType.MESH
F32 = jnp.float32
BF16 = jnp.bfloat16
NT = (((1,), (1,)), ((), ()))
LANE = 128


def silu(v):
    return v / (1.0 + jnp.exp(-v))


def dot(a, b):
    return jnp.dot(a, b, preferred_element_type=F32)


def dot_nt(a, b):
    return lax.dot_general(a, b, NT, preferred_element_type=F32)


def rope_rows(length, rows):
    lane = lax.broadcasted_iota(jnp.int32, (rows, HEAD_SIZE), 1)
    token = lax.broadcasted_iota(jnp.int32, (rows, HEAD_SIZE), 0)
    pair = lax.rem(lane, HEAD_SIZE // 2).astype(F32)
    angle = (token + length).astype(F32) * jnp.exp(pair * (-2.0 * math.log(10000.0) / HEAD_SIZE))
    turns = jnp.floor(angle * (2.0 / math.pi) + 0.5)
    rest = angle - turns * 1.5703125
    rest = rest - turns * 4.837512969970703125e-4
    rest = rest - turns * 7.54978995489188216e-8
    z = rest * rest
    sine = ((-1.9515295891e-4 * z + 8.3321608736e-3) * z - 1.6666654611e-1) * z * rest + rest
    cosine = (2.443315711809948e-5 * z - 1.388731625493765e-3) * z + 4.166664568298827e-2
    cosine = cosine * z * z - 0.5 * z + 1.0
    quarter = turns - 4.0 * jnp.floor(turns * 0.25)
    odd = (quarter == 1.0) | (quarter == 3.0)
    cos_t = jnp.where(odd, sine, cosine)
    cos_t = jnp.where((quarter == 1.0) | (quarter == 2.0), -cos_t, cos_t)
    sin_t = jnp.where(odd, cosine, sine)
    sin_t = jnp.where(quarter >= 2.0, -sin_t, sin_t)
    return cos_t, jnp.where(lane < HEAD_SIZE // 2, -sin_t, sin_t)


def fused_kernel(
    dims,
    tokens, gain_h, bias_h, rate_h, skip_h, lengths_h, mixer_gain_h,
    mixer_in, shared_in, step_in, keys, values, state, mixer_out, gate, up, down,
    out,
    gain, bias, rate, skip, lengths, mixer_gain,
    w_a, w_b, k_v, v_v, s_v, g_v, u_v, m_v, d_v,
    xg, xf, xb, sq_send, sq_recv, p_send, p_recv, c_b, tot, step_f,
    f_send, f_recv, feat, bc, qbuf, knbuf, vnbuf, obuf, cbuf, rbuf, own,
    m_send, m_recv, lhs, gsc, gu_send, gu_recv, hbuf, o_send, o_recv,
    sem_w, sem_loc, sem_gs, sem_gr, sem_ps, sem_pr, sem_fs, sem_fr,
    sem_ms, sem_mr, sem_us, sem_ur, sem_hs, sem_hr, sem_os, sem_or,
):
    n, n_short, rows, width, gcol, scol, ncol, ocol, fspans, ospans = dims
    n_chunk = len(fspans)
    n_oc = len(ospans)
    total_rows = n * rows
    me = lax.axis_index("wide")
    s = lax.axis_index("short")
    other = 1 - s
    q_heads = QUERY_HEADS // n_short
    kv_heads = KEY_VALUE_HEADS // n_short
    m_heads = MH // n_short
    rep = QUERY_HEADS // KEY_VALUE_HEADS
    acol = gcol + scol + ncol
    fpad = xpad(gcol)
    opad = round_up(ocol)

    def peer(d):
        return lax.rem(me + d, n)

    weights = []

    def fetch(src, dst):
        copy = pltpu.make_async_copy(src, dst, sem_w.at[len(weights)])
        copy.start()
        weights.append(copy)
        return copy

    barrier = pltpu.get_barrier_semaphore()
    for d in range(n):
        for e in range(n_short):
            if d or e:
                pl.semaphore_signal(
                    barrier, inc=1,
                    device_id={"wide": peer(d), "short": lax.rem(s + e, n_short)},
                    device_id_type=MESH,
                )
    own_tokens = fetch(tokens, xg.at[me])
    small = [
        fetch(gain_h, gain), fetch(bias_h, bias), fetch(rate_h, rate), fetch(skip_h, skip),
        fetch(lengths_h, lengths), fetch(mixer_gain_h, mixer_gain),
    ]
    fa = [
        fetch(mixer_in.at[other], w_a.at[pl.ds(0, gcol)]),
        fetch(shared_in, w_a.at[pl.ds(gcol, scol)]),
        fetch(step_in, w_a.at[pl.ds(gcol + scol, ncol)]),
    ]
    fb = [fetch(mixer_in.at[s], w_b)]

    def cols(c):
        return pl.ds(*fspans[c])

    fgu = []
    for c in range(n_chunk):
        fgu.append(
            (fetch(gate.at[:, cols(c)], g_v.at[:, cols(c)]), fetch(up.at[:, cols(c)], u_v.at[:, cols(c)]))
        )
        if c == 0:
            fkv = [fetch(keys, k_v), fetch(values, v_v), fetch(state, s_v)]
    fdn = [fetch(down.at[cols(c)], d_v.at[cols(c)]) for c in range(n_chunk)]
    fmo = [fetch(mixer_out.at[g], m_v.at[g, pl.ds(0, ocol)]) for g in range(n_short)]

    for g in range(n_short):
        if opad > ocol:
            m_v[g, ocol:opad, :] = jnp.zeros((opad - ocol, width), BF16)
    feat[...] = jnp.zeros_like(feat)
    bc[...] = jnp.zeros_like(bc)
    qbuf[...] = jnp.zeros_like(qbuf)
    knbuf[...] = jnp.zeros_like(knbuf)
    vnbuf[...] = jnp.zeros_like(vnbuf)
    cbuf[...] = jnp.zeros_like(cbuf)
    c_b[...] = jnp.zeros_like(c_b)
    tot[...] = jnp.zeros_like(tot)
    own[...] = jnp.zeros_like(own)
    own_tokens.wait()
    pl.semaphore_wait(barrier, n * n_short - 1)

    def remote(src, dst, send, recv, wide, short):
        copy = pltpu.make_async_remote_copy(
            src_ref=src, dst_ref=dst, send_sem=send, recv_sem=recv,
            device_id={"wide": wide, "short": short}, device_id_type=MESH,
        )
        copy.start()
        return copy

    def arrived(buf, recv):
        pltpu.make_async_copy(buf, buf, recv).wait()

    sent = []

    for d in range(1, n):
        sent.append(remote(xg.at[me], xg.at[me], sem_gs.at[d], sem_gr.at[me], peer(d), s))
    for copy in small:
        copy.wait()
    cos_t, sin_t = rope_rows(lengths[...], rows)
    for d in range(1, n):
        arrived(xg.at[peer(d)], sem_gr.at[peer(d)])
    for j in range(n):
        xf[rows * j : rows * (j + 1), :] = xg[j].astype(F32)
    x = xf[...]
    sq_send[...] = jnp.broadcast_to(jnp.sum(x * x, axis=1, keepdims=True), sq_send.shape)
    sent.append(remote(sq_send, sq_recv, sem_ps.at[0], sem_pr.at[0], me, other))
    for j in range(width // LANE):
        lanes = slice(j * LANE, (j + 1) * LANE)
        xb[:, lanes] = (xf[:, lanes] * gain[j : j + 1, :]).astype(BF16)

    for copy in fa:
        copy.wait()
    p_send[...] = dot_nt(xb[...], w_a[...])
    sent.append(remote(p_send, p_recv, sem_ps.at[1], sem_pr.at[1], me, other))
    fb[0].wait()
    c_b[:, :gcol] = dot_nt(xb[...], w_b[...])
    lane = lax.broadcasted_iota(jnp.int32, (total_rows, acol), 1)
    mine = jnp.where(lane < gcol, c_b[:, :acol], p_send[...])
    arrived(sq_recv, sem_pr.at[0])
    mean_square = (sq_send[:, :1] + sq_recv[:, :1]) / D
    inv = lax.rsqrt(mean_square + epsilon)
    arrived(p_recv, sem_pr.at[1])
    tot[:, :acol] = (mine + p_recv[...]) * inv
    whole = tot[...]
    wide_lane = lax.broadcasted_iota(jnp.int32, whole.shape, 1)
    span = whole.shape[1]
    features = pltpu.roll(
        jnp.where(wide_lane < gcol, whole, 0.0), lax.rem(me * gcol, LANE), 1
    )
    low = pltpu.roll(whole, span - gcol, 1)[:, :LANE]
    low_lane = lax.broadcasted_iota(jnp.int32, low.shape, 1)
    low = pltpu.roll(jnp.where(low_lane < scol, low, 0.0), lax.rem(me * scol, LANE), 1)
    step_all = pltpu.roll(whole, span - gcol - scol, 1)[:, :LANE]
    step_f[...] = pltpu.roll(step_all, lax.rem(LANE - s * m_heads, LANE), 1)
    tot[...] = features
    c_b[:, :LANE] = low
    for r in range(n):
        f_send[r, :, :fpad] = tot[rows * r : rows * (r + 1), :].astype(BF16)
        f_send[r, :, fpad:] = c_b[rows * r : rows * (r + 1), :LANE].astype(BF16)
    for d in range(1, n):
        to = peer(d)
        sent.append(remote(f_send.at[to], f_recv.at[me], sem_fs.at[d], sem_fr.at[me], to, s))
    own_f = pltpu.make_async_copy(f_send.at[me], f_recv.at[me], sem_loc.at[0])
    own_f.start()

    half = total_rows // n_short

    def gate_up(c):
        part = slice(fspans[c][0], fspans[c][0] + fspans[c][1])
        fgu[c][0].wait()
        both = [dot(xb[...], g_v[:, part])]
        fgu[c][1].wait()
        both.append(dot(xb[...], u_v[:, part]))
        for k in range(2):
            for i in range(n_short):
                gsc[k, i, :, part] = both[k][half * i : half * (i + 1)] * inv[half * i : half * (i + 1)]
        for k in range(2):
            gu_send[k, :, part] = gsc[k, other, :, part].astype(BF16)
        sent.append(
            remote(
                gu_send.at[:, :, cols(c)], gu_recv.at[:, :, cols(c)], sem_us.at[c], sem_ur.at[c], me, other
            )
        )

    def hidden(c):
        part = slice(fspans[c][0], fspans[c][0] + fspans[c][1])
        arrived(gu_recv.at[:, :, cols(c)], sem_ur.at[c])
        a = gsc[0, s, :, part] + gu_recv[0, :, part].astype(F32)
        b = gsc[1, s, :, part] + gu_recv[1, :, part].astype(F32)
        hbuf[s, :, part] = (silu(a) * b).astype(BF16)
        sent.append(
            remote(
                hbuf.at[s, :, cols(c)], hbuf.at[s, :, cols(c)], sem_hs.at[c], sem_hr.at[c], me, other
            )
        )

    def down_part(c):
        part = slice(fspans[c][0], fspans[c][0] + fspans[c][1])
        arrived(hbuf.at[other, :, cols(c)], sem_hr.at[c])
        fdn[c].wait()
        term = dot(hbuf[:, :, part].reshape(total_rows, fspans[c][1]), d_v[part, :])
        xf[...] = term if c == 0 else xf[...] + term

    early = max(1, n_chunk - 1)
    for c in range(early):
        gate_up(c)
        if c:
            hidden(c - 1)

    own_f.wait()
    for d in range(1, n):
        arrived(f_recv.at[peer(d)], sem_fr.at[peer(d)])
    fwidth = feat.shape[1]
    for j in range(n):
        base = gcol * j // LANE * LANE
        w = min(fpad, fwidth - base)
        feat[:, base : base + w] += f_recv[j, :, :w].astype(F32)
        base = scol * j // LANE * LANE
        bc[:, base : base + LANE] += f_recv[j, :, fpad:].astype(F32)
    for copy in fkv:
        copy.wait()
    k_at = q_heads * HEAD_SIZE
    v_at = k_at + kv_heads * HEAD_SIZE
    x_at = v_at + kv_heads * HEAD_SIZE
    z_at = x_at + m_heads * MP

    def turn(v):
        return v * cos_t + jnp.concatenate([v[:, HEAD_SIZE // 2 :], v[:, : HEAD_SIZE // 2]], axis=1) * sin_t

    length = lengths[...]
    for kv in range(kv_heads):
        for i in range(rep):
            h = kv * rep + i
            qbuf[kv, rows * i : rows * (i + 1), :] = turn(feat[:, h * HEAD_SIZE : (h + 1) * HEAD_SIZE])
        knbuf[kv, :rows, :] = turn(feat[:, k_at + kv * HEAD_SIZE : k_at + (kv + 1) * HEAD_SIZE])
        vnbuf[kv, :rows, :] = feat[:, v_at + kv * HEAD_SIZE : v_at + (kv + 1) * HEAD_SIZE]
        head = slice(kv * HEAD_SIZE, (kv + 1) * HEAD_SIZE)
        query = qbuf[kv].astype(BF16)
        scale = HEAD_SIZE ** (-0.5)
        old = dot_nt(query, k_v[:, head]) * scale
        new = dot_nt(query, knbuf[kv].astype(BF16)) * scale
        slot = lax.broadcasted_iota(jnp.int32, old.shape, 1)
        old = jnp.where(slot < length, old, -1e30)
        token = lax.rem(lax.broadcasted_iota(jnp.int32, new.shape, 0), rows)
        fresh = lax.broadcasted_iota(jnp.int32, new.shape, 1)
        new = jnp.where(fresh <= token, new, -1e30)
        top = jnp.maximum(
            jnp.max(old, axis=1, keepdims=True), jnp.max(new, axis=1, keepdims=True)
        )
        old = jnp.exp(old - top)
        new = jnp.exp(new - top)
        den = jnp.sum(old, axis=1, keepdims=True) + jnp.sum(new, axis=1, keepdims=True)
        obuf[kv] = dot((old / den).astype(BF16), v_v[:, head]) + dot(
            (new / den).astype(BF16), vnbuf[kv].astype(BF16)
        )
        for i in range(rep):
            h = kv * rep + i
            own[:, h * HEAD_SIZE : (h + 1) * HEAD_SIZE] = obuf[kv, rows * i : rows * (i + 1), :]

    write = silu(bc[:, :NS])
    read = silu(bc[:, NS:])
    rest = read
    for i in range(3):
        piece = rest.astype(BF16).astype(F32)
        cbuf[rows * i : rows * (i + 1), :] = piece
        rest = rest - piece
    rbuf[...] = dot_nt(cbuf[...].astype(BF16), s_v[...])
    carried = rbuf[:rows] + rbuf[rows : 2 * rows] + rbuf[2 * rows : 3 * rows]
    raw = step_f[pl.ds(rows * me, rows), :][:, :m_heads] + bias[...]
    step = jnp.maximum(raw, 0.0) + jnp.log1p(jnp.exp(-jnp.abs(raw)))
    run = [step[:1]]
    for t in range(1, rows):
        run.append(run[-1] + step[t : t + 1])
    age = jnp.concatenate(run, axis=0) * rate[...]
    kept = jnp.exp(-age)
    tid = lax.broadcasted_iota(jnp.int32, age.shape, 0)
    mix = []
    for u in range(rows):
        overlap = jnp.sum(read * write[u : u + 1], axis=1, keepdims=True)
        fade = jnp.exp(-jnp.maximum(age - age[u : u + 1], 0.0))
        mix.append(jnp.where(tid >= u, fade, 0.0) * step[u : u + 1] * overlap)
    skips = skip[...]
    for h in range(m_heads):
        hs = slice(h * MP, (h + 1) * MP)
        active = silu(feat[:, x_at + h * MP : x_at + (h + 1) * MP])
        y = kept[:, h : h + 1] * carried[:, hs] + skips[:, h : h + 1] * active
        for u in range(rows):
            y = y + mix[u][:, h : h + 1] * active[u : u + 1]
        y = y * silu(feat[:, z_at + h * MP : z_at + (h + 1) * MP])
        ms = jnp.mean(y * y, axis=1, keepdims=True)
        at = (q_heads + h) * MP
        own[:, at : at + MP] = y * lax.rsqrt(ms + epsilon) * mixer_gain[:, hs]

    window = opad + LANE
    for j in range(n):
        base = ocol * j // LANE * LANE
        off = ocol * j - base
        v = own[:, base : base + window]
        if off:
            v = jnp.concatenate([v[:, off:], v[:, :off]], axis=1)
        m_send[j] = v[:, :opad].astype(BF16)
    for d in range(n):
        to = peer(d)
        for e in range(n_short):
            if d or e:
                sent.append(
                    remote(
                        m_send.at[to], m_recv.at[s, me], sem_ms.at[d, e], sem_mr.at[s, me],
                        to, lax.rem(s + e, n_short),
                    )
                )
    own_m = pltpu.make_async_copy(m_send.at[me], m_recv.at[s, me], sem_loc.at[1])
    own_m.start()

    for c in range(early, n_chunk):
        gate_up(c)
        hidden(c - 1)
    for c in range(n_chunk):
        if c == max(0, n_chunk - 2):
            hidden(n_chunk - 1)
        down_part(c)
    own_m.wait()
    for d in range(n):
        for e in range(n_short):
            if d or e:
                g = lax.rem(s + e, n_short)
                arrived(m_recv.at[g, peer(d)], sem_mr.at[g, peer(d)])
    for g in range(n_short):
        for j in range(n):
            lhs[g, rows * j : rows * (j + 1), :] = m_recv[g, j].astype(F32)
    for copy in fmo:
        copy.wait()
    for o in range(n_oc):
        oc = slice(ospans[o][0], ospans[o][0] + ospans[o][1])
        acc = xf[:, oc]
        for g in range(n_short):
            acc = acc + dot(lhs[g].astype(BF16), m_v[g, :, oc])
        xf[:, oc] = acc
        for r in range(n):
            o_send[r, :, oc] = xf[rows * r : rows * (r + 1), oc].astype(BF16)
        for k in range(n - 1):
            to = jnp.where(me <= k, k + 1, k)
            part = pl.ds(*ospans[o])
            sent.append(
                remote(
                    o_send.at[to, :, part], o_recv.at[me, :, part], sem_os.at[o, k], sem_or.at[o, me], to, s
                )
            )
    for o in range(n_oc):
        part = pl.ds(*ospans[o])
        oc = slice(ospans[o][0], ospans[o][0] + ospans[o][1])
        acc = xg[me, :, oc].astype(F32) + o_send[me, :, oc].astype(F32)
        for d in range(1, n):
            arrived(o_recv.at[peer(d), :, part], sem_or.at[o, peer(d)])
            acc = acc + o_recv[peer(d), :, oc].astype(F32)
        out[:, oc] = acc.astype(BF16)
    for copy in sent:
        copy.wait_send()


def round_up(v):
    return -(-v // LANE) * LANE


def xpad(gcol):
    return round_up(gcol + LANE - 1)


def spans_of(width, piece):
    return tuple((at, min(piece, width - at)) for at in range(0, width, piece))


def fused(*args):
    (tokens, norm_gain, mixer_in, shared_in, step_in, step_bias, decay_rate, skip_gain,
     cached_keys, cached_values, lengths, state_cache, mixer_gain, mixer_out,
     gate_weight, up_weight, down_weight) = args
    n = lax.axis_size("wide")
    n_short = lax.axis_size("short")
    rows, width = tokens.shape
    gcol = mixer_in.shape[2]
    scol = shared_in.shape[1]
    ncol = step_in.shape[1]
    ocol = mixer_out.shape[1]
    ffl = gate_weight.shape[1]
    fspans = spans_of(ffl, 1024)
    ospans = spans_of(width, 512)
    n_chunk = len(fspans)
    n_oc = len(ospans)
    m_heads = MH // n_short
    kv_heads = KEY_VALUE_HEADS // n_short
    total_rows = n * rows
    acol = gcol + scol + ncol
    fpad = xpad(gcol)
    opad = round_up(ocol)
    features = n * gcol
    outs = n * ocol
    half = total_rows // n_short
    dims = (n, n_short, rows, width, gcol, scol, ncol, ocol, fspans, ospans)
    vm = pl.BlockSpec(memory_space=pltpu.VMEM)
    hb = pl.BlockSpec(memory_space=pl.ANY)
    V = pltpu.VMEM
    dma = pltpu.SemaphoreType.DMA
    kvw = cached_keys.shape[2]
    slots = cached_keys.shape[1]
    scratch = [
        V((width // LANE, LANE), F32), V((1, m_heads), F32), V((1, m_heads), F32),
        V((1, m_heads), F32), V((1, 1), jnp.int32), V((1, m_heads * MP), F32),
        V((acol, width), BF16), V((gcol, width), BF16), V((slots, kvw), BF16),
        V((slots, kvw), BF16), V((m_heads * MP, NS), BF16),
        V((width, ffl), BF16), V((width, ffl), BF16),
        V((n_short, opad, width), BF16), V((ffl, width), BF16),
        V((n, rows, width), BF16), V((total_rows, width), F32), V((total_rows, width), BF16),
        V((total_rows, LANE), F32), V((total_rows, LANE), F32),
        V((total_rows, acol), F32), V((total_rows, acol), F32), V((total_rows, fpad), F32),
        V((total_rows, fpad), F32), V((total_rows, LANE), F32),
        V((n, rows, fpad + LANE), BF16), V((n, rows, fpad + LANE), BF16),
        V((rows, features), F32), V((rows, 2 * NS), F32),
        V((kv_heads, 32, HEAD_SIZE), F32), V((kv_heads, 16, HEAD_SIZE), F32),
        V((kv_heads, 16, HEAD_SIZE), F32), V((kv_heads, 32, HEAD_SIZE), F32),
        V((16, NS), F32), V((16, m_heads * MP), F32),
        V((rows, round_up(outs) + opad + LANE), F32),
        V((n, rows, opad), BF16), V((n_short, n, rows, opad), BF16),
        V((n_short, total_rows, opad), F32),
        V((2, n_short, half, ffl), F32),
        V((2, half, ffl), BF16), V((2, half, ffl), BF16),
        V((n_short, half, ffl), BF16),
        V((n, rows, width), BF16), V((n, rows, width), BF16),
        dma((7 + 4 + 3 * n_chunk + 3 + n_short,)), dma((2,)),
        dma((n,)), dma((n,)), dma((2,)), dma((2,)), dma((n,)), dma((n,)),
        dma((n, n_short)), dma((n_short, n)), dma((n_chunk,)), dma((n_chunk,)),
        dma((n_chunk,)), dma((n_chunk,)), dma((n_oc, n)), dma((n_oc, n)),
    ]
    return pl.pallas_call(
        functools.partial(fused_kernel, dims),
        out_shape=pltpu.VMEM((rows, width), BF16),
        in_specs=[hb] * 17,
        out_specs=vm,
        scratch_shapes=scratch,
        name="layer",
        compiler_params=pltpu.CompilerParams(
            collective_id=0, has_side_effects=True, vmem_limit_bytes=66 * 1000 * 1000
        ),
    )(
        tokens, norm_gain.reshape(width // LANE, LANE), step_bias[None, :], decay_rate[None, :],
        skip_gain[None, :], lengths[None, :], mixer_gain[None, :],
        jnp.transpose(mixer_in, (1, 2, 0)), shared_in.T, step_in.T,
        cached_keys[0], cached_values[0], state_cache.reshape(m_heads * MP, NS),
        mixer_out, gate_weight, up_weight, down_weight,
    )


def fits(n, n_short, args):
    tokens, mixer_in, shared_in, step_in = args[0], args[2], args[3], args[4]
    return (
        n_short == 2
        and tokens.shape[0] == DRAFT_TOKENS
        and n * DRAFT_TOKENS == 32
        and mixer_in.shape[2] % 16 == 0
        and shared_in.shape[1] % 16 == 0
        and LANE % shared_in.shape[1] == 0
        and step_in.shape[1] % 16 == 0
        and args[13].shape[1] % 16 == 0
        and args[14].shape[1] % LANE == 0
        and tokens.shape[1] % LANE == 0
    )


def layer(*args):
    if fits(lax.axis_size("wide"), lax.axis_size("short"), args):
        return fused(*args)
    return on_device(*args)


def solution(mesh):
    in_specs = (
        P(("groups", "wide"), "short"),
        P("short"),
        P("short", None, "wide"),
        P("short", "wide"),
        P("short", None),
        P("short"),
        P("short"),
        P("short"),
        P(("groups", "wide"), None, "short"),
        P(("groups", "wide"), None, "short"),
        P(("groups", "wide")),
        P(("groups", "wide"), "short", None, None),
        P("short"),
        P(None, "wide", "short"),
        P("short", "wide"),
        P("short", "wide"),
        P("wide", "short"),
    )
    out_specs = P(("groups", "wide"), "short")
    return jax.shard_map(
        layer, mesh=mesh, in_specs=in_specs, out_specs=out_specs, check_vma=False
    )
```

```python
import functools
import math
import jax
import jax.numpy as jnp
from jax import lax
from jax.experimental import pallas as pl
from jax.experimental.pallas import tpu as pltpu
from jax.sharding import PartitionSpec as P

D = 5120
QUERY_HEADS = 20
KEY_VALUE_HEADS = 4
HEAD_SIZE = 128
MH = 32
MP = 128
NS = 256
CACHE_SLOTS = 512
DRAFT_TOKENS = 4


epsilon = 1e-05


def as_sent(x):

    def short(part):
        return part.astype(jnp.bfloat16) if part.dtype == jnp.float32 else part

    return jax.tree.map(short, x)


def rotate(vectors, cos_table, sin_table):
    half_width = vectors.shape[-1] // 2
    first_half = vectors[..., :half_width]
    second_half = vectors[..., half_width:]
    return jnp.concatenate(
        [
            first_half * cos_table - second_half * sin_table,
            second_half * cos_table + first_half * sin_table,
        ],
        axis=-1,
    )


def rope_tables(positions):
    frequency = 10000.0 ** (-(jnp.arange(HEAD_SIZE // 2, dtype=jnp.float32) * 2.0 / HEAD_SIZE))
    angles = positions.astype(jnp.float32)[..., None] * frequency
    return (jnp.cos(angles), jnp.sin(angles))


def attend_one(queries, fresh_keys, fresh_values, key_tile_block, value_tile_block, length):
    score_scale = HEAD_SIZE ** (-0.5)
    scores_cache = (
        jnp.einsum("tkgd,pkd->kgtp", queries, key_tile_block, preferred_element_type=jnp.float32)
        * score_scale
    )
    scores_new = (
        jnp.einsum("tkgd,ukd->kgtu", queries, fresh_keys, preferred_element_type=jnp.float32)
        * score_scale
    )
    live_keys = jnp.arange(key_tile_block.shape[0], dtype=jnp.int32) < length
    causal = jnp.arange(DRAFT_TOKENS)[None, :] <= jnp.arange(DRAFT_TOKENS)[:, None]
    scores_cache = jnp.where(live_keys, scores_cache, -1e30)
    scores_new = jnp.where(causal, scores_new, -1e30)
    highest = jnp.maximum(jnp.max(scores_cache, axis=-1), jnp.max(scores_new, axis=-1))[..., None]
    weight_cache = jnp.exp(scores_cache - highest)
    weight_new = jnp.exp(scores_new - highest)
    denominator = jnp.sum(weight_cache, axis=-1, keepdims=True) + jnp.sum(
        weight_new, axis=-1, keepdims=True
    )
    probs_cache = (weight_cache / denominator).astype(jnp.bfloat16)
    probs_new = (weight_new / denominator).astype(jnp.bfloat16)
    attended = jnp.einsum(
        "kgtp,pkd->tkgd", probs_cache, value_tile_block, preferred_element_type=jnp.float32
    )
    attended = attended + jnp.einsum(
        "kgtu,ukd->tkgd", probs_new, fresh_values, preferred_element_type=jnp.float32
    )
    return attended.astype(jnp.bfloat16)


def scan_one(
    state_block, inputs_x, gates_z, b_vals, c_vals, step_sizes, decay_rates, skip_gain, head_gain
):
    hstate = state_block.astype(jnp.float32)
    in_active = jax.nn.silu(inputs_x.astype(jnp.float32))
    write_vec = jax.nn.silu(b_vals.astype(jnp.float32))
    read_vec = jax.nn.silu(c_vals.astype(jnp.float32))
    outputs = []
    for draft_index in range(DRAFT_TOKENS):
        decays = jnp.exp(-step_sizes[draft_index] * decay_rates)
        inject = (step_sizes[draft_index][:, None] * in_active[draft_index])[
            :, :, None
        ] * write_vec[draft_index][None, None, :]
        hstate = decays[:, None, None] * hstate + inject
        readout = jnp.einsum(
            "hpn,n->hp", hstate, read_vec[draft_index], precision=lax.Precision.HIGHEST
        )
        outputs.append(readout + skip_gain[:, None] * in_active[draft_index])
    gated = jnp.stack(outputs) * jax.nn.silu(gates_z.astype(jnp.float32))
    mean_square = jnp.mean(gated * gated, axis=-1, keepdims=True)
    return (gated * lax.rsqrt(mean_square + epsilon) * head_gain).astype(jnp.bfloat16)


def on_device(
    tokens,
    norm_gain,
    mixer_in,
    shared_in,
    step_in,
    step_bias,
    decay_rate,
    skip_gain,
    cached_keys,
    cached_values,
    lengths,
    state_cache,
    mixer_gain,
    mixer_out,
    gate_weight,
    up_weight,
    down_weight,
):
    short_count = lax.axis_size("short")
    n_wide = lax.axis_size("wide")
    q_heads = QUERY_HEADS // short_count
    key_value_heads = KEY_VALUE_HEADS // short_count
    ssm_heads = MH // short_count
    repeat_factor = QUERY_HEADS // KEY_VALUE_HEADS
    query_size = q_heads * HEAD_SIZE
    key_size = key_value_heads * HEAD_SIZE
    m_size = ssm_heads * MP
    local_rows = tokens.shape[0]
    requests = local_rows // DRAFT_TOKENS
    width_half = tokens.shape[1]
    rows_float = tokens.astype(jnp.float32)
    square_sum = lax.psum(jnp.sum(rows_float * rows_float, axis=1), "short")
    inv_rms = lax.rsqrt(square_sum / D + epsilon)
    normed = (rows_float * inv_rms[:, None] * norm_gain[None, :]).astype(jnp.bfloat16)
    step_terms = jnp.dot(normed, step_in, preferred_element_type=jnp.float32)
    step_raw = lax.psum_scatter(step_terms, "short", scatter_dimension=1, tiled=True)
    gathered = lax.all_gather(normed, "wide", axis=0, tiled=True)
    group_part = jnp.einsum("rd,dgc->rgc", gathered, mixer_in, preferred_element_type=jnp.float32)
    shared_part = jnp.dot(gathered, shared_in, preferred_element_type=jnp.float32)[:, None, :]
    gate_part = jnp.dot(gathered, gate_weight, preferred_element_type=jnp.float32)
    up_part = jnp.dot(gathered, up_weight, preferred_element_type=jnp.float32)
    gate_half, up_half = (
        lax.psum_scatter(
            gate_part.astype(jnp.bfloat16), "short", scatter_dimension=0, tiled=True
        ).astype(jnp.float32),
        lax.psum_scatter(
            up_part.astype(jnp.bfloat16), "short", scatter_dimension=0, tiled=True
        ).astype(jnp.float32),
    )
    hidden_half = (jax.nn.silu(gate_half) * up_half).astype(jnp.bfloat16)
    hidden = lax.all_gather(hidden_half, "short", axis=0, tiled=True)
    group_moved, shared_moved = (
        lax.all_to_all(group_part, "wide", split_axis=0, concat_axis=2, tiled=True),
        lax.all_to_all(shared_part, "wide", split_axis=0, concat_axis=2, tiled=True),
    )
    group_sum = lax.psum_scatter(group_moved, "short", scatter_dimension=1, tiled=True)
    shared_sum = lax.psum(shared_moved, "short")
    features = group_sum[:, 0, :].astype(jnp.bfloat16)
    shared_vals = shared_sum[:, 0, :].astype(jnp.bfloat16)
    queries = features[:, :query_size].reshape(requests, DRAFT_TOKENS, q_heads, HEAD_SIZE)
    fresh_keys = features[:, query_size : query_size + key_size].reshape(
        requests, DRAFT_TOKENS, key_value_heads, HEAD_SIZE
    )
    fresh_values = features[:, query_size + key_size : query_size + 2 * key_size].reshape(
        requests, DRAFT_TOKENS, key_value_heads, HEAD_SIZE
    )
    x_start = query_size + 2 * key_size
    inputs_x = features[:, x_start : x_start + m_size].reshape(
        requests, DRAFT_TOKENS, ssm_heads, MP
    )
    gates_z = features[:, x_start + m_size : x_start + 2 * m_size].reshape(
        requests, DRAFT_TOKENS, ssm_heads, MP
    )
    positions = lengths[:, None] + jnp.arange(DRAFT_TOKENS, dtype=jnp.int32)[None, :]
    cos_table, sin_table = rope_tables(positions)
    cos_table = cos_table[:, :, None, :]
    sin_table = sin_table[:, :, None, :]
    rotated_queries = rotate(queries.astype(jnp.float32), cos_table, sin_table).astype(jnp.bfloat16)
    keys_rot = rotate(fresh_keys.astype(jnp.float32), cos_table, sin_table).astype(jnp.bfloat16)
    rotated_queries = rotated_queries.reshape(
        requests, DRAFT_TOKENS, key_value_heads, repeat_factor, HEAD_SIZE
    )
    key_tile_block = cached_keys.reshape(requests, CACHE_SLOTS, key_value_heads, HEAD_SIZE)
    value_tile_block = cached_values.reshape(requests, CACHE_SLOTS, key_value_heads, HEAD_SIZE)
    attention = jax.vmap(attend_one)(
        rotated_queries, keys_rot, fresh_values, key_tile_block, value_tile_block, lengths
    )
    step_sizes = jax.nn.softplus(
        step_raw.reshape(requests, DRAFT_TOKENS, ssm_heads) + step_bias[None, None, :]
    )
    b_vals = shared_vals[:, :NS].reshape(requests, DRAFT_TOKENS, NS)
    c_vals = shared_vals[:, NS:].reshape(requests, DRAFT_TOKENS, NS)
    head_gain = mixer_gain.reshape(ssm_heads, MP)
    mamba = jax.vmap(scan_one, in_axes=(0, 0, 0, 0, 0, 0, None, None, None))(
        state_cache, inputs_x, gates_z, b_vals, c_vals, step_sizes, decay_rate, skip_gain, head_gain
    )
    own_rows = jnp.concatenate(
        [attention.reshape(local_rows, query_size), mamba.reshape(local_rows, m_size)], axis=1
    )
    returned = lax.all_to_all(
        as_sent(own_rows[:, None, :]), "wide", split_axis=2, concat_axis=0, tiled=True
    )
    both_groups = lax.all_gather(as_sent(returned), "short", axis=1, tiled=True).astype(
        returned.dtype
    )
    projected = jnp.einsum(
        "rgc,gcd->rd", both_groups, mixer_out, preferred_element_type=jnp.float32
    )
    summed = projected + jnp.dot(hidden, down_weight, preferred_element_type=jnp.float32)
    pieces = lax.all_to_all(
        summed.reshape(n_wide, local_rows, width_half).astype(jnp.bfloat16),
        "wide",
        split_axis=0,
        concat_axis=0,
        tiled=True,
    ).astype(jnp.float32)
    total = rows_float + jnp.sum(pieces, axis=0)
    return total.astype(jnp.bfloat16)


MESH = pl.DeviceIdType.MESH
F32 = jnp.float32
BF16 = jnp.bfloat16
NT = (((1,), (1,)), ((), ()))
LANE = 128


def silu(v):
    return v / (1.0 + jnp.exp(-v))


def dot(a, b):
    return jnp.dot(a, b, preferred_element_type=F32)


def dot_nt(a, b):
    return lax.dot_general(a, b, NT, preferred_element_type=F32)


def rope_rows(length, rows):
    lane = lax.broadcasted_iota(jnp.int32, (rows, HEAD_SIZE), 1)
    token = lax.broadcasted_iota(jnp.int32, (rows, HEAD_SIZE), 0)
    pair = lax.rem(lane, HEAD_SIZE // 2).astype(F32)
    angle = (token + length).astype(F32) * jnp.exp(pair * (-2.0 * math.log(10000.0) / HEAD_SIZE))
    turns = jnp.floor(angle * (2.0 / math.pi) + 0.5)
    rest = angle - turns * 1.5703125
    rest = rest - turns * 4.837512969970703125e-4
    rest = rest - turns * 7.54978995489188216e-8
    z = rest * rest
    sine = ((-1.9515295891e-4 * z + 8.3321608736e-3) * z - 1.6666654611e-1) * z * rest + rest
    cosine = (2.443315711809948e-5 * z - 1.388731625493765e-3) * z + 4.166664568298827e-2
    cosine = cosine * z * z - 0.5 * z + 1.0
    quarter = turns - 4.0 * jnp.floor(turns * 0.25)
    odd = (quarter == 1.0) | (quarter == 3.0)
    cos_t = jnp.where(odd, sine, cosine)
    cos_t = jnp.where((quarter == 1.0) | (quarter == 2.0), -cos_t, cos_t)
    sin_t = jnp.where(odd, cosine, sine)
    sin_t = jnp.where(quarter >= 2.0, -sin_t, sin_t)
    return cos_t, jnp.where(lane < HEAD_SIZE // 2, -sin_t, sin_t)


def fused_kernel(
    dims,
    tokens, gain_h, bias_h, rate_h, skip_h, lengths, mixer_gain_h,
    mixer_in, shared_in, step_in, keys, values, state, mixer_out, gate, up, down,
    out,
    gain, bias, rate, skip, mixer_gain,
    w_a, w_b, k_v, v_v, s_v, g_v, u_v, m_v, d_v,
    xg, xf, xb, sq_send, sq_recv, p_send, p_recv, c_b, tot, step_f,
    f_send, f_recv, feat, bc, qbuf, knbuf, vnbuf, obuf, cbuf, rbuf, own,
    m_send, m_recv, lhs, gsc, gu_send, gu_recv, hbuf, o_send, o_recv,
    sem_w, sem_loc, sem_gs, sem_gr, sem_ps, sem_pr, sem_fs, sem_fr,
    sem_ms, sem_mr, sem_us, sem_ur, sem_hs, sem_hr, sem_os, sem_or,
):
    n, n_short, rows, width, gcol, scol, ncol, ocol, fspans, ospans = dims
    n_chunk = len(fspans)
    n_oc = len(ospans)
    total_rows = n * rows
    me = lax.axis_index("wide")
    s = lax.axis_index("short")
    other = 1 - s
    q_heads = QUERY_HEADS // n_short
    kv_heads = KEY_VALUE_HEADS // n_short
    m_heads = MH // n_short
    rep = QUERY_HEADS // KEY_VALUE_HEADS
    acol = gcol + scol + ncol
    fpad = xpad(gcol)
    opad = round_up(ocol)

    def peer(d):
        return lax.rem(me + d, n)

    def upward(k):
        return jnp.where(me <= k, k + 1, k)

    def far_first(k):
        down_to = n - 1 - k
        return jnp.where(2 * me >= n, upward(k), jnp.where(down_to > me, down_to, down_to - 1))

    weights = []

    def fetch(src, dst):
        copy = pltpu.make_async_copy(src, dst, sem_w.at[len(weights)])
        copy.start()
        weights.append(copy)
        return copy

    barrier = pltpu.get_barrier_semaphore()
    for k in range(n):
        for e in range(n_short):
            if k < n - 1 or e:
                pl.semaphore_signal(
                    barrier, inc=1,
                    device_id={
                        "wide": far_first(k) if k < n - 1 else me, "short": lax.rem(s + e, n_short)
                    },
                    device_id_type=MESH,
                )
    own_tokens = fetch(tokens, xg.at[me])
    small = [
        fetch(gain_h, gain), fetch(bias_h, bias), fetch(rate_h, rate), fetch(skip_h, skip),
        fetch(mixer_gain_h, mixer_gain),
    ]
    fa = [
        fetch(mixer_in.at[other], w_a.at[pl.ds(0, gcol)]),
        fetch(shared_in, w_a.at[pl.ds(gcol, scol)]),
        fetch(step_in, w_a.at[pl.ds(gcol + scol, ncol)]),
    ]
    fb = [fetch(mixer_in.at[s], w_b)]

    def cols(c):
        return pl.ds(*fspans[c])

    fgu = []
    for c in range(n_chunk):
        fgu.append(
            (fetch(gate.at[:, cols(c)], g_v.at[:, cols(c)]), fetch(up.at[:, cols(c)], u_v.at[:, cols(c)]))
        )
        if c == 0:
            fkv = [fetch(keys, k_v), fetch(values, v_v), fetch(state, s_v)]
    fdn = [fetch(down.at[cols(c)], d_v.at[cols(c)]) for c in range(n_chunk)]
    fmo = [fetch(mixer_out.at[g], m_v.at[g, pl.ds(0, ocol)]) for g in range(n_short)]

    for g in range(n_short):
        if opad > ocol:
            m_v[g, ocol:opad, :] = jnp.zeros((opad - ocol, width), BF16)
    feat[...] = jnp.zeros_like(feat)
    bc[...] = jnp.zeros_like(bc)
    qbuf[...] = jnp.zeros_like(qbuf)
    knbuf[...] = jnp.zeros_like(knbuf)
    vnbuf[...] = jnp.zeros_like(vnbuf)
    cbuf[...] = jnp.zeros_like(cbuf)
    c_b[...] = jnp.zeros_like(c_b)
    tot[...] = jnp.zeros_like(tot)
    own[...] = jnp.zeros_like(own)
    own_tokens.wait()
    pl.semaphore_wait(barrier, n * n_short - 1)

    def remote(src, dst, send, recv, wide, short):
        copy = pltpu.make_async_remote_copy(
            src_ref=src, dst_ref=dst, send_sem=send, recv_sem=recv,
            device_id={"wide": wide, "short": short}, device_id_type=MESH,
        )
        copy.start()
        return copy

    def arrived(buf, recv):
        pltpu.make_async_copy(buf, buf, recv).wait()

    sent = []

    for k in range(n - 1):
        remote(xg.at[me], xg.at[me], sem_gs, sem_gr, far_first(k), s)
    for copy in small:
        copy.wait()
    cos_t, sin_t = rope_rows(lengths[0], rows)
    arrived(xg.at[pl.ds(0, n - 1)], sem_gr)
    for j in range(n):
        xf[rows * j : rows * (j + 1), :] = xg[j].astype(F32)
    x = xf[...]
    sq_send[...] = jnp.broadcast_to(jnp.sum(x * x, axis=1, keepdims=True), sq_send.shape)
    sent.append(remote(sq_send, sq_recv, sem_ps.at[0], sem_pr.at[0], me, other))
    for j in range(width // LANE):
        lanes = slice(j * LANE, (j + 1) * LANE)
        xb[:, lanes] = (xf[:, lanes] * gain[j : j + 1, :]).astype(BF16)

    for copy in fa:
        copy.wait()
    p_send[...] = dot_nt(xb[...], w_a[...])
    sent.append(remote(p_send, p_recv, sem_ps.at[1], sem_pr.at[1], me, other))
    fb[0].wait()
    c_b[:, :gcol] = dot_nt(xb[...], w_b[...])
    lane = lax.broadcasted_iota(jnp.int32, (total_rows, acol), 1)
    mine = jnp.where(lane < gcol, c_b[:, :acol], p_send[...])
    arrived(sq_recv, sem_pr.at[0])
    mean_square = (sq_send[:, :1] + sq_recv[:, :1]) / D
    inv = lax.rsqrt(mean_square + epsilon)
    arrived(p_recv, sem_pr.at[1])
    tot[:, :acol] = (mine + p_recv[...]) * inv
    whole = tot[...]
    wide_lane = lax.broadcasted_iota(jnp.int32, whole.shape, 1)
    span = whole.shape[1]
    features = pltpu.roll(
        jnp.where(wide_lane < gcol, whole, 0.0), lax.rem(me * gcol, LANE), 1
    )
    low = pltpu.roll(whole, span - gcol, 1)[:, :LANE]
    low_lane = lax.broadcasted_iota(jnp.int32, low.shape, 1)
    low = pltpu.roll(jnp.where(low_lane < scol, low, 0.0), lax.rem(me * scol, LANE), 1)
    step_all = pltpu.roll(whole, span - gcol - scol, 1)[:, :LANE]
    step_f[...] = pltpu.roll(step_all, lax.rem(LANE - s * m_heads, LANE), 1)
    tot[...] = features
    c_b[:, :LANE] = low
    for r in range(n):
        f_send[r, :, :fpad] = tot[rows * r : rows * (r + 1), :].astype(BF16)
        f_send[r, :, fpad:] = c_b[rows * r : rows * (r + 1), :LANE].astype(BF16)
    for k in range(n - 1):
        to = far_first(k)
        remote(f_send.at[to], f_recv.at[me], sem_fs, sem_fr, to, s)
    own_f = pltpu.make_async_copy(f_send.at[me], f_recv.at[me], sem_loc.at[0])
    own_f.start()

    half = total_rows // n_short

    def gate_up(c):
        part = slice(fspans[c][0], fspans[c][0] + fspans[c][1])
        fgu[c][0].wait()
        both = [dot(xb[...], g_v[:, part])]
        fgu[c][1].wait()
        both.append(dot(xb[...], u_v[:, part]))
        for k in range(2):
            for i in range(n_short):
                gsc[k, i, :, part] = both[k][half * i : half * (i + 1)] * inv[half * i : half * (i + 1)]
        for k in range(2):
            gu_send[k, :, part] = gsc[k, other, :, part].astype(BF16)
        sent.append(
            remote(
                gu_send.at[:, :, cols(c)], gu_recv.at[:, :, cols(c)], sem_us.at[c], sem_ur.at[c], me, other
            )
        )

    def hidden(c):
        part = slice(fspans[c][0], fspans[c][0] + fspans[c][1])
        arrived(gu_recv.at[:, :, cols(c)], sem_ur.at[c])
        a = gsc[0, s, :, part] + gu_recv[0, :, part].astype(F32)
        b = gsc[1, s, :, part] + gu_recv[1, :, part].astype(F32)
        hbuf[s, :, part] = (silu(a) * b).astype(BF16)
        sent.append(
            remote(
                hbuf.at[s, :, cols(c)], hbuf.at[s, :, cols(c)], sem_hs.at[c], sem_hr.at[c], me, other
            )
        )

    def down_part(c):
        part = slice(fspans[c][0], fspans[c][0] + fspans[c][1])
        arrived(hbuf.at[other, :, cols(c)], sem_hr.at[c])
        fdn[c].wait()
        term = dot(hbuf[:, :, part].reshape(total_rows, fspans[c][1]), d_v[part, :])
        xf[...] = term if c == 0 else xf[...] + term

    early = max(1, n_chunk - 1)
    for c in range(early):
        gate_up(c)
        if c:
            hidden(c - 1)

    own_f.wait()
    arrived(f_recv.at[pl.ds(0, n - 1)], sem_fr)
    fwidth = feat.shape[1]
    for j in range(n):
        base = gcol * j // LANE * LANE
        w = min(fpad, fwidth - base)
        feat[:, base : base + w] += f_recv[j, :, :w].astype(F32)
        base = scol * j // LANE * LANE
        bc[:, base : base + LANE] += f_recv[j, :, fpad:].astype(F32)
    for copy in fkv:
        copy.wait()
    k_at = q_heads * HEAD_SIZE
    v_at = k_at + kv_heads * HEAD_SIZE
    x_at = v_at + kv_heads * HEAD_SIZE
    z_at = x_at + m_heads * MP

    def turn(v):
        return v * cos_t + jnp.concatenate([v[:, HEAD_SIZE // 2 :], v[:, : HEAD_SIZE // 2]], axis=1) * sin_t

    length = lengths[0]
    for kv in range(kv_heads):
        for i in range(rep):
            h = kv * rep + i
            qbuf[kv, rows * i : rows * (i + 1), :] = turn(feat[:, h * HEAD_SIZE : (h + 1) * HEAD_SIZE])
        knbuf[kv, :rows, :] = turn(feat[:, k_at + kv * HEAD_SIZE : k_at + (kv + 1) * HEAD_SIZE])
        vnbuf[kv, :rows, :] = feat[:, v_at + kv * HEAD_SIZE : v_at + (kv + 1) * HEAD_SIZE]
        head = slice(kv * HEAD_SIZE, (kv + 1) * HEAD_SIZE)
        query = qbuf[kv].astype(BF16)
        scale = HEAD_SIZE ** (-0.5)
        old = dot_nt(query, k_v[:, head]) * scale
        new = dot_nt(query, knbuf[kv].astype(BF16)) * scale
        slot = lax.broadcasted_iota(jnp.int32, old.shape, 1)
        old = jnp.where(slot < length, old, -1e30)
        token = lax.rem(lax.broadcasted_iota(jnp.int32, new.shape, 0), rows)
        fresh = lax.broadcasted_iota(jnp.int32, new.shape, 1)
        new = jnp.where(fresh <= token, new, -1e30)
        top = jnp.maximum(
            jnp.max(old, axis=1, keepdims=True), jnp.max(new, axis=1, keepdims=True)
        )
        old = jnp.exp(old - top)
        new = jnp.exp(new - top)
        den = jnp.sum(old, axis=1, keepdims=True) + jnp.sum(new, axis=1, keepdims=True)
        obuf[kv] = dot((old / den).astype(BF16), v_v[:, head]) + dot(
            (new / den).astype(BF16), vnbuf[kv].astype(BF16)
        )
        for i in range(rep):
            h = kv * rep + i
            own[:, h * HEAD_SIZE : (h + 1) * HEAD_SIZE] = obuf[kv, rows * i : rows * (i + 1), :]

    write = silu(bc[:, :NS])
    read = silu(bc[:, NS:])
    rest = read
    for i in range(3):
        piece = rest.astype(BF16).astype(F32)
        cbuf[rows * i : rows * (i + 1), :] = piece
        rest = rest - piece
    rbuf[...] = dot_nt(cbuf[...].astype(BF16), s_v[...])
    carried = rbuf[:rows] + rbuf[rows : 2 * rows] + rbuf[2 * rows : 3 * rows]
    raw = step_f[pl.ds(rows * me, rows), :][:, :m_heads] + bias[...]
    step = jnp.maximum(raw, 0.0) + jnp.log1p(jnp.exp(-jnp.abs(raw)))
    run = [step[:1]]
    for t in range(1, rows):
        run.append(run[-1] + step[t : t + 1])
    age = jnp.concatenate(run, axis=0) * rate[...]
    kept = jnp.exp(-age)
    tid = lax.broadcasted_iota(jnp.int32, age.shape, 0)
    mix = []
    for u in range(rows):
        overlap = jnp.sum(read * write[u : u + 1], axis=1, keepdims=True)
        fade = jnp.exp(-jnp.maximum(age - age[u : u + 1], 0.0))
        mix.append(jnp.where(tid >= u, fade, 0.0) * step[u : u + 1] * overlap)
    skips = skip[...]
    for h in range(m_heads):
        hs = slice(h * MP, (h + 1) * MP)
        active = silu(feat[:, x_at + h * MP : x_at + (h + 1) * MP])
        y = kept[:, h : h + 1] * carried[:, hs] + skips[:, h : h + 1] * active
        for u in range(rows):
            y = y + mix[u][:, h : h + 1] * active[u : u + 1]
        y = y * silu(feat[:, z_at + h * MP : z_at + (h + 1) * MP])
        ms = jnp.mean(y * y, axis=1, keepdims=True)
        at = (q_heads + h) * MP
        own[:, at : at + MP] = y * lax.rsqrt(ms + epsilon) * mixer_gain[:, hs]

    window = opad + LANE
    for j in range(n):
        base = ocol * j // LANE * LANE
        off = ocol * j - base
        v = own[:, base : base + window]
        if off:
            v = jnp.concatenate([v[:, off:], v[:, :off]], axis=1)
        m_send[j] = v[:, :opad].astype(BF16)
    for k in range(n):
        to = far_first(k) if k < n - 1 else me
        for e in range(n_short):
            if k < n - 1 or e:
                remote(
                    m_send.at[to], m_recv.at[s * n + me], sem_ms, sem_mr, to, lax.rem(s + e, n_short)
                )
    own_m = pltpu.make_async_copy(m_send.at[me], m_recv.at[s * n + me], sem_loc.at[1])
    own_m.start()

    for c in range(early, n_chunk):
        gate_up(c)
        hidden(c - 1)
    for c in range(n_chunk):
        if c == max(0, n_chunk - 2):
            hidden(n_chunk - 1)
        down_part(c)
    own_m.wait()
    arrived(m_recv.at[pl.ds(0, n * n_short - 1)], sem_mr)
    for g in range(n_short):
        for j in range(n):
            lhs[g, rows * j : rows * (j + 1), :] = m_recv[g * n + j].astype(F32)
    for copy in fmo:
        copy.wait()
    for o in range(n_oc):
        oc = slice(ospans[o][0], ospans[o][0] + ospans[o][1])
        acc = xf[:, oc]
        for g in range(n_short):
            acc = acc + dot(lhs[g].astype(BF16), m_v[g, :, oc])
        xf[:, oc] = acc
        for r in range(n):
            o_send[r, :, oc] = xf[rows * r : rows * (r + 1), oc].astype(BF16)
        for k in range(n - 1):
            to = upward(k)
            part = pl.ds(*ospans[o])
            remote(o_send.at[to, :, part], o_recv.at[me, :, part], sem_os.at[o], sem_or.at[o], to, s)
    for o in range(n_oc):
        part = pl.ds(*ospans[o])
        oc = slice(ospans[o][0], ospans[o][0] + ospans[o][1])
        acc = xg[me, :, oc].astype(F32) + o_send[me, :, oc].astype(F32)
        arrived(o_recv.at[pl.ds(0, n - 1), :, part], sem_or.at[o])
        for d in range(1, n):
            acc = acc + o_recv[peer(d), :, oc].astype(F32)
        out[:, oc] = acc.astype(BF16)
    for copy in sent:
        copy.wait_send()
    arrived(xg.at[pl.ds(0, n - 1)], sem_gs)
    arrived(f_send.at[pl.ds(0, n - 1)], sem_fs)
    arrived(m_recv.at[pl.ds(0, n * n_short - 1)], sem_ms)
    for o in range(n_oc):
        arrived(o_send.at[pl.ds(0, n - 1), :, pl.ds(*ospans[o])], sem_os.at[o])


def round_up(v):
    return -(-v // LANE) * LANE


def xpad(gcol):
    return round_up(gcol + LANE - 1)


def spans_of(width, piece):
    return tuple((at, min(piece, width - at)) for at in range(0, width, piece))


def fused(*args):
    (tokens, norm_gain, mixer_in, shared_in, step_in, step_bias, decay_rate, skip_gain,
     cached_keys, cached_values, lengths, state_cache, mixer_gain, mixer_out,
     gate_weight, up_weight, down_weight) = args
    n = lax.axis_size("wide")
    n_short = lax.axis_size("short")
    rows, width = tokens.shape
    gcol = mixer_in.shape[2]
    scol = shared_in.shape[1]
    ncol = step_in.shape[1]
    ocol = mixer_out.shape[1]
    ffl = gate_weight.shape[1]
    fspans = spans_of(ffl, 1024)
    first = min(512, width)
    ospans = ((0, first),) + tuple((first + at, size) for at, size in spans_of(width - first, 1024))
    n_chunk = len(fspans)
    n_oc = len(ospans)
    m_heads = MH // n_short
    kv_heads = KEY_VALUE_HEADS // n_short
    total_rows = n * rows
    acol = gcol + scol + ncol
    fpad = xpad(gcol)
    opad = round_up(ocol)
    features = n * gcol
    outs = n * ocol
    half = total_rows // n_short
    dims = (n, n_short, rows, width, gcol, scol, ncol, ocol, fspans, ospans)
    vm = pl.BlockSpec(memory_space=pltpu.VMEM)
    hb = pl.BlockSpec(memory_space=pl.ANY)
    V = pltpu.VMEM
    dma = pltpu.SemaphoreType.DMA
    kvw = cached_keys.shape[2]
    slots = cached_keys.shape[1]
    scratch = [
        V((width // LANE, LANE), F32), V((1, m_heads), F32), V((1, m_heads), F32),
        V((1, m_heads), F32), V((1, m_heads * MP), F32),
        V((acol, width), BF16), V((gcol, width), BF16), V((slots, kvw), BF16),
        V((slots, kvw), BF16), V((m_heads * MP, NS), BF16),
        V((width, ffl), BF16), V((width, ffl), BF16),
        V((n_short, opad, width), BF16), V((ffl, width), BF16),
        V((n, rows, width), BF16), V((total_rows, width), F32), V((total_rows, width), BF16),
        V((total_rows, LANE), F32), V((total_rows, LANE), F32),
        V((total_rows, acol), F32), V((total_rows, acol), F32), V((total_rows, fpad), F32),
        V((total_rows, fpad), F32), V((total_rows, LANE), F32),
        V((n, rows, fpad + LANE), BF16), V((n, rows, fpad + LANE), BF16),
        V((rows, features), F32), V((rows, 2 * NS), F32),
        V((kv_heads, 32, HEAD_SIZE), F32), V((kv_heads, 16, HEAD_SIZE), F32),
        V((kv_heads, 16, HEAD_SIZE), F32), V((kv_heads, 32, HEAD_SIZE), F32),
        V((16, NS), F32), V((16, m_heads * MP), F32),
        V((rows, round_up(outs) + opad + LANE), F32),
        V((n, rows, opad), BF16), V((n_short * n, rows, opad), BF16),
        V((n_short, total_rows, opad), F32),
        V((2, n_short, half, ffl), F32),
        V((2, half, ffl), BF16), V((2, half, ffl), BF16),
        V((n_short, half, ffl), BF16),
        V((n, rows, width), BF16), V((n, rows, width), BF16),
        dma((6 + 4 + 3 * n_chunk + 3 + n_short,)), dma((2,)),
        dma, dma, dma((2,)), dma((2,)), dma, dma,
        dma, dma, dma((n_chunk,)), dma((n_chunk,)),
        dma((n_chunk,)), dma((n_chunk,)), dma((n_oc,)), dma((n_oc,)),
    ]
    return pl.pallas_call(
        functools.partial(fused_kernel, dims),
        out_shape=pltpu.VMEM((rows, width), BF16),
        in_specs=[hb] * 5 + [pl.BlockSpec(memory_space=pltpu.SMEM)] + [hb] * 11,
        out_specs=vm,
        scratch_shapes=scratch,
        name="layer",
        compiler_params=pltpu.CompilerParams(
            collective_id=0, has_side_effects=True, vmem_limit_bytes=66 * 1000 * 1000
        ),
    )(
        tokens, norm_gain.reshape(width // LANE, LANE), step_bias[None, :], decay_rate[None, :],
        skip_gain[None, :], lengths, mixer_gain[None, :],
        jnp.transpose(mixer_in, (1, 2, 0)), shared_in.T, step_in.T,
        cached_keys[0], cached_values[0], state_cache.reshape(m_heads * MP, NS),
        mixer_out, gate_weight, up_weight, down_weight,
    )


def fits(n, n_short, args):
    tokens, mixer_in, shared_in, step_in = args[0], args[2], args[3], args[4]
    return (
        n_short == 2
        and tokens.shape[0] == DRAFT_TOKENS
        and n * DRAFT_TOKENS == 32
        and mixer_in.shape[2] % 16 == 0
        and shared_in.shape[1] % 16 == 0
        and LANE % shared_in.shape[1] == 0
        and step_in.shape[1] % 16 == 0
        and args[13].shape[1] % 16 == 0
        and args[14].shape[1] % LANE == 0
        and tokens.shape[1] % LANE == 0
    )


def layer(*args):
    if fits(lax.axis_size("wide"), lax.axis_size("short"), args):
        return fused(*args)
    return on_device(*args)


def solution(mesh):
    in_specs = (
        P(("groups", "wide"), "short"),
        P("short"),
        P("short", None, "wide"),
        P("short", "wide"),
        P("short", None),
        P("short"),
        P("short"),
        P("short"),
        P(("groups", "wide"), None, "short"),
        P(("groups", "wide"), None, "short"),
        P(("groups", "wide")),
        P(("groups", "wide"), "short", None, None),
        P("short"),
        P(None, "wide", "short"),
        P("short", "wide"),
        P("short", "wide"),
        P("wide", "short"),
    )
    out_specs = P(("groups", "wide"), "short")
    return jax.shard_map(
        layer, mesh=mesh, in_specs=in_specs, out_specs=out_specs, check_vma=False
    )
```

```python
import functools
import math
import jax
import jax.numpy as jnp
from jax import lax
from jax.experimental import pallas as pl
from jax.experimental.pallas import tpu as pltpu
from jax.sharding import PartitionSpec as P

D = 5120
QUERY_HEADS = 20
KEY_VALUE_HEADS = 4
HEAD_SIZE = 128
MH = 32
MP = 128
NS = 256
CACHE_SLOTS = 512
DRAFT_TOKENS = 4


epsilon = 1e-05


def as_sent(x):

    def short(part):
        return part.astype(jnp.bfloat16) if part.dtype == jnp.float32 else part

    return jax.tree.map(short, x)


def rotate(vectors, cos_table, sin_table):
    half_width = vectors.shape[-1] // 2
    first_half = vectors[..., :half_width]
    second_half = vectors[..., half_width:]
    return jnp.concatenate(
        [
            first_half * cos_table - second_half * sin_table,
            second_half * cos_table + first_half * sin_table,
        ],
        axis=-1,
    )


def rope_tables(positions):
    frequency = 10000.0 ** (-(jnp.arange(HEAD_SIZE // 2, dtype=jnp.float32) * 2.0 / HEAD_SIZE))
    angles = positions.astype(jnp.float32)[..., None] * frequency
    return (jnp.cos(angles), jnp.sin(angles))


def attend_one(queries, fresh_keys, fresh_values, key_tile_block, value_tile_block, length):
    score_scale = HEAD_SIZE ** (-0.5)
    scores_cache = (
        jnp.einsum("tkgd,pkd->kgtp", queries, key_tile_block, preferred_element_type=jnp.float32)
        * score_scale
    )
    scores_new = (
        jnp.einsum("tkgd,ukd->kgtu", queries, fresh_keys, preferred_element_type=jnp.float32)
        * score_scale
    )
    live_keys = jnp.arange(key_tile_block.shape[0], dtype=jnp.int32) < length
    causal = jnp.arange(DRAFT_TOKENS)[None, :] <= jnp.arange(DRAFT_TOKENS)[:, None]
    scores_cache = jnp.where(live_keys, scores_cache, -1e30)
    scores_new = jnp.where(causal, scores_new, -1e30)
    highest = jnp.maximum(jnp.max(scores_cache, axis=-1), jnp.max(scores_new, axis=-1))[..., None]
    weight_cache = jnp.exp(scores_cache - highest)
    weight_new = jnp.exp(scores_new - highest)
    denominator = jnp.sum(weight_cache, axis=-1, keepdims=True) + jnp.sum(
        weight_new, axis=-1, keepdims=True
    )
    probs_cache = (weight_cache / denominator).astype(jnp.bfloat16)
    probs_new = (weight_new / denominator).astype(jnp.bfloat16)
    attended = jnp.einsum(
        "kgtp,pkd->tkgd", probs_cache, value_tile_block, preferred_element_type=jnp.float32
    )
    attended = attended + jnp.einsum(
        "kgtu,ukd->tkgd", probs_new, fresh_values, preferred_element_type=jnp.float32
    )
    return attended.astype(jnp.bfloat16)


def scan_one(
    state_block, inputs_x, gates_z, b_vals, c_vals, step_sizes, decay_rates, skip_gain, head_gain
):
    hstate = state_block.astype(jnp.float32)
    in_active = jax.nn.silu(inputs_x.astype(jnp.float32))
    write_vec = jax.nn.silu(b_vals.astype(jnp.float32))
    read_vec = jax.nn.silu(c_vals.astype(jnp.float32))
    outputs = []
    for draft_index in range(DRAFT_TOKENS):
        decays = jnp.exp(-step_sizes[draft_index] * decay_rates)
        inject = (step_sizes[draft_index][:, None] * in_active[draft_index])[
            :, :, None
        ] * write_vec[draft_index][None, None, :]
        hstate = decays[:, None, None] * hstate + inject
        readout = jnp.einsum(
            "hpn,n->hp", hstate, read_vec[draft_index], precision=lax.Precision.HIGHEST
        )
        outputs.append(readout + skip_gain[:, None] * in_active[draft_index])
    gated = jnp.stack(outputs) * jax.nn.silu(gates_z.astype(jnp.float32))
    mean_square = jnp.mean(gated * gated, axis=-1, keepdims=True)
    return (gated * lax.rsqrt(mean_square + epsilon) * head_gain).astype(jnp.bfloat16)


def on_device(
    tokens,
    norm_gain,
    mixer_in,
    shared_in,
    step_in,
    step_bias,
    decay_rate,
    skip_gain,
    cached_keys,
    cached_values,
    lengths,
    state_cache,
    mixer_gain,
    mixer_out,
    gate_weight,
    up_weight,
    down_weight,
):
    short_count = lax.axis_size("short")
    n_wide = lax.axis_size("wide")
    q_heads = QUERY_HEADS // short_count
    key_value_heads = KEY_VALUE_HEADS // short_count
    ssm_heads = MH // short_count
    repeat_factor = QUERY_HEADS // KEY_VALUE_HEADS
    query_size = q_heads * HEAD_SIZE
    key_size = key_value_heads * HEAD_SIZE
    m_size = ssm_heads * MP
    local_rows = tokens.shape[0]
    requests = local_rows // DRAFT_TOKENS
    width_half = tokens.shape[1]
    rows_float = tokens.astype(jnp.float32)
    square_sum = lax.psum(jnp.sum(rows_float * rows_float, axis=1), "short")
    inv_rms = lax.rsqrt(square_sum / D + epsilon)
    normed = (rows_float * inv_rms[:, None] * norm_gain[None, :]).astype(jnp.bfloat16)
    step_terms = jnp.dot(normed, step_in, preferred_element_type=jnp.float32)
    step_raw = lax.psum_scatter(step_terms, "short", scatter_dimension=1, tiled=True)
    gathered = lax.all_gather(normed, "wide", axis=0, tiled=True)
    group_part = jnp.einsum("rd,dgc->rgc", gathered, mixer_in, preferred_element_type=jnp.float32)
    shared_part = jnp.dot(gathered, shared_in, preferred_element_type=jnp.float32)[:, None, :]
    gate_part = jnp.dot(gathered, gate_weight, preferred_element_type=jnp.float32)
    up_part = jnp.dot(gathered, up_weight, preferred_element_type=jnp.float32)
    gate_half, up_half = (
        lax.psum_scatter(
            gate_part.astype(jnp.bfloat16), "short", scatter_dimension=0, tiled=True
        ).astype(jnp.float32),
        lax.psum_scatter(
            up_part.astype(jnp.bfloat16), "short", scatter_dimension=0, tiled=True
        ).astype(jnp.float32),
    )
    hidden_half = (jax.nn.silu(gate_half) * up_half).astype(jnp.bfloat16)
    hidden = lax.all_gather(hidden_half, "short", axis=0, tiled=True)
    group_moved, shared_moved = (
        lax.all_to_all(group_part, "wide", split_axis=0, concat_axis=2, tiled=True),
        lax.all_to_all(shared_part, "wide", split_axis=0, concat_axis=2, tiled=True),
    )
    group_sum = lax.psum_scatter(group_moved, "short", scatter_dimension=1, tiled=True)
    shared_sum = lax.psum(shared_moved, "short")
    features = group_sum[:, 0, :].astype(jnp.bfloat16)
    shared_vals = shared_sum[:, 0, :].astype(jnp.bfloat16)
    queries = features[:, :query_size].reshape(requests, DRAFT_TOKENS, q_heads, HEAD_SIZE)
    fresh_keys = features[:, query_size : query_size + key_size].reshape(
        requests, DRAFT_TOKENS, key_value_heads, HEAD_SIZE
    )
    fresh_values = features[:, query_size + key_size : query_size + 2 * key_size].reshape(
        requests, DRAFT_TOKENS, key_value_heads, HEAD_SIZE
    )
    x_start = query_size + 2 * key_size
    inputs_x = features[:, x_start : x_start + m_size].reshape(
        requests, DRAFT_TOKENS, ssm_heads, MP
    )
    gates_z = features[:, x_start + m_size : x_start + 2 * m_size].reshape(
        requests, DRAFT_TOKENS, ssm_heads, MP
    )
    positions = lengths[:, None] + jnp.arange(DRAFT_TOKENS, dtype=jnp.int32)[None, :]
    cos_table, sin_table = rope_tables(positions)
    cos_table = cos_table[:, :, None, :]
    sin_table = sin_table[:, :, None, :]
    rotated_queries = rotate(queries.astype(jnp.float32), cos_table, sin_table).astype(jnp.bfloat16)
    keys_rot = rotate(fresh_keys.astype(jnp.float32), cos_table, sin_table).astype(jnp.bfloat16)
    rotated_queries = rotated_queries.reshape(
        requests, DRAFT_TOKENS, key_value_heads, repeat_factor, HEAD_SIZE
    )
    key_tile_block = cached_keys.reshape(requests, CACHE_SLOTS, key_value_heads, HEAD_SIZE)
    value_tile_block = cached_values.reshape(requests, CACHE_SLOTS, key_value_heads, HEAD_SIZE)
    attention = jax.vmap(attend_one)(
        rotated_queries, keys_rot, fresh_values, key_tile_block, value_tile_block, lengths
    )
    step_sizes = jax.nn.softplus(
        step_raw.reshape(requests, DRAFT_TOKENS, ssm_heads) + step_bias[None, None, :]
    )
    b_vals = shared_vals[:, :NS].reshape(requests, DRAFT_TOKENS, NS)
    c_vals = shared_vals[:, NS:].reshape(requests, DRAFT_TOKENS, NS)
    head_gain = mixer_gain.reshape(ssm_heads, MP)
    mamba = jax.vmap(scan_one, in_axes=(0, 0, 0, 0, 0, 0, None, None, None))(
        state_cache, inputs_x, gates_z, b_vals, c_vals, step_sizes, decay_rate, skip_gain, head_gain
    )
    own_rows = jnp.concatenate(
        [attention.reshape(local_rows, query_size), mamba.reshape(local_rows, m_size)], axis=1
    )
    returned = lax.all_to_all(
        as_sent(own_rows[:, None, :]), "wide", split_axis=2, concat_axis=0, tiled=True
    )
    both_groups = lax.all_gather(as_sent(returned), "short", axis=1, tiled=True).astype(
        returned.dtype
    )
    projected = jnp.einsum(
        "rgc,gcd->rd", both_groups, mixer_out, preferred_element_type=jnp.float32
    )
    summed = projected + jnp.dot(hidden, down_weight, preferred_element_type=jnp.float32)
    pieces = lax.all_to_all(
        summed.reshape(n_wide, local_rows, width_half).astype(jnp.bfloat16),
        "wide",
        split_axis=0,
        concat_axis=0,
        tiled=True,
    ).astype(jnp.float32)
    total = rows_float + jnp.sum(pieces, axis=0)
    return total.astype(jnp.bfloat16)


MESH = pl.DeviceIdType.MESH
F32 = jnp.float32
BF16 = jnp.bfloat16
NT = (((1,), (1,)), ((), ()))
LANE = 128


def silu(v):
    return v / (1.0 + jnp.exp(-v))


def dot(a, b):
    return jnp.dot(a, b, preferred_element_type=F32)


def dot_nt(a, b):
    return lax.dot_general(a, b, NT, preferred_element_type=F32)


def rope_rows(length, rows):
    lane = lax.broadcasted_iota(jnp.int32, (rows, HEAD_SIZE), 1)
    token = lax.broadcasted_iota(jnp.int32, (rows, HEAD_SIZE), 0)
    pair = lax.rem(lane, HEAD_SIZE // 2).astype(F32)
    angle = (token + length).astype(F32) * jnp.exp(pair * (-2.0 * math.log(10000.0) / HEAD_SIZE))
    turns = jnp.floor(angle * (2.0 / math.pi) + 0.5)
    rest = angle - turns * 1.5703125
    rest = rest - turns * 4.837512969970703125e-4
    rest = rest - turns * 7.54978995489188216e-8
    z = rest * rest
    sine = ((-1.9515295891e-4 * z + 8.3321608736e-3) * z - 1.6666654611e-1) * z * rest + rest
    cosine = (2.443315711809948e-5 * z - 1.388731625493765e-3) * z + 4.166664568298827e-2
    cosine = cosine * z * z - 0.5 * z + 1.0
    quarter = turns - 4.0 * jnp.floor(turns * 0.25)
    odd = (quarter == 1.0) | (quarter == 3.0)
    cos_t = jnp.where(odd, sine, cosine)
    cos_t = jnp.where((quarter == 1.0) | (quarter == 2.0), -cos_t, cos_t)
    sin_t = jnp.where(odd, cosine, sine)
    sin_t = jnp.where(quarter >= 2.0, -sin_t, sin_t)
    return cos_t, jnp.where(lane < HEAD_SIZE // 2, -sin_t, sin_t)


def fused_kernel(
    dims,
    tokens, gain_h, bias_h, rate_h, skip_h, lengths, mixer_gain_h,
    mixer_in, shared_in, step_in, keys, values, state, mixer_out, gate, up, down,
    out,
    gain, bias, rate, skip, mixer_gain,
    w_a, w_b, k_v, v_v, s_v, g_v, u_v, m_v, d_v,
    xg, xf, xb, sq_send, sq_recv, p_send, p_recv, c_b, tot, step_f,
    f_send, f_recv, feat, bc, qbuf, knbuf, vnbuf, obuf, cbuf, rbuf, own,
    m_send, m_recv, lhs, gsc, gu_send, gu_recv, hbuf, o_send, o_recv,
    sem_w, sem_loc, sem_gs, sem_gr, sem_ps, sem_pr, sem_fs, sem_fr,
    sem_ms, sem_mr, sem_us, sem_ur, sem_hs, sem_hr, sem_os, sem_or,
):
    n, n_short, rows, width, gcol, scol, ncol, ocol, fspans, ospans = dims
    n_chunk = len(fspans)
    n_oc = len(ospans)
    total_rows = n * rows
    me = lax.axis_index("wide")
    s = lax.axis_index("short")
    other = 1 - s
    q_heads = QUERY_HEADS // n_short
    kv_heads = KEY_VALUE_HEADS // n_short
    m_heads = MH // n_short
    rep = QUERY_HEADS // KEY_VALUE_HEADS
    acol = gcol + scol + ncol
    fpad = xpad(gcol)
    opad = round_up(ocol)

    def peer(d):
        return lax.rem(me + d, n)

    def upward(k):
        return jnp.where(me <= k, k + 1, k)

    def far_first(k):
        down_to = n - 1 - k
        return jnp.where(2 * me >= n, upward(k), jnp.where(down_to > me, down_to, down_to - 1))

    weights = []

    def fetch(src, dst):
        copy = pltpu.make_async_copy(src, dst, sem_w.at[len(weights)])
        copy.start()
        weights.append(copy)
        return copy

    barrier = pltpu.get_barrier_semaphore()
    for k in range(n):
        for e in range(n_short):
            if k < n - 1 or e:
                pl.semaphore_signal(
                    barrier, inc=1,
                    device_id={
                        "wide": far_first(k) if k < n - 1 else me, "short": lax.rem(s + e, n_short)
                    },
                    device_id_type=MESH,
                )
    own_tokens = fetch(tokens, xg.at[me])
    small = [
        fetch(gain_h, gain), fetch(bias_h, bias), fetch(rate_h, rate), fetch(skip_h, skip),
        fetch(mixer_gain_h, mixer_gain),
    ]
    lead = dims_lead(gcol)
    fa = [
        fetch(mixer_in.at[s, pl.ds(0, lead)], w_a.at[pl.ds(0, lead)]),
        fetch(mixer_in.at[other], w_a.at[pl.ds(lead, gcol)]),
        fetch(shared_in, w_a.at[pl.ds(lead + gcol, scol)]),
        fetch(step_in, w_a.at[pl.ds(lead + gcol + scol, ncol)]),
    ]
    fb = [fetch(mixer_in.at[s, pl.ds(lead, gcol - lead)], w_b)]

    def cols(c):
        return pl.ds(*fspans[c])

    fgu = []
    for c in range(n_chunk):
        fgu.append(
            (fetch(gate.at[:, cols(c)], g_v.at[:, cols(c)]), fetch(up.at[:, cols(c)], u_v.at[:, cols(c)]))
        )
        if c == 0:
            fkv = [fetch(keys, k_v), fetch(values, v_v), fetch(state, s_v)]
    fdn = [fetch(down.at[cols(c)], d_v.at[cols(c)]) for c in range(n_chunk)]
    fmo = [fetch(mixer_out.at[g], m_v.at[g, pl.ds(0, ocol)]) for g in range(n_short)]

    own_tokens.wait()
    pl.semaphore_wait(barrier, n * n_short - 1)

    def remote(src, dst, send, recv, wide, short):
        copy = pltpu.make_async_remote_copy(
            src_ref=src, dst_ref=dst, send_sem=send, recv_sem=recv,
            device_id={"wide": wide, "short": short}, device_id_type=MESH,
        )
        copy.start()
        return copy

    def arrived(buf, recv):
        pltpu.make_async_copy(buf, buf, recv).wait()

    sent = []

    for k in range(n - 1):
        remote(xg.at[me], xg.at[me], sem_gs, sem_gr, far_first(k), s)
    for g in range(n_short):
        if opad > ocol:
            m_v[g, ocol:opad, :] = jnp.zeros((opad - ocol, width), BF16)
    feat[...] = jnp.zeros_like(feat)
    bc[...] = jnp.zeros_like(bc)
    qbuf[...] = jnp.zeros_like(qbuf)
    knbuf[...] = jnp.zeros_like(knbuf)
    vnbuf[...] = jnp.zeros_like(vnbuf)
    cbuf[...] = jnp.zeros_like(cbuf)
    c_b[...] = jnp.zeros_like(c_b)
    tot[...] = jnp.zeros_like(tot)
    own[...] = jnp.zeros_like(own)
    for copy in small:
        copy.wait()
    cos_t, sin_t = rope_rows(lengths[0], rows)
    arrived(xg.at[pl.ds(0, n - 1)], sem_gr)
    for j in range(n):
        xf[rows * j : rows * (j + 1), :] = xg[j].astype(F32)
    x = xf[...]
    sq_send[...] = jnp.broadcast_to(jnp.sum(x * x, axis=1, keepdims=True), sq_send.shape)
    sent.append(remote(sq_send, sq_recv, sem_ps.at[0], sem_pr.at[0], me, other))
    for j in range(width // LANE):
        lanes = slice(j * LANE, (j + 1) * LANE)
        xb[:, lanes] = (xf[:, lanes] * gain[j : j + 1, :]).astype(BF16)

    for copy in fa:
        copy.wait()
    both = dot_nt(xb[...], w_a[...])
    p_send[...] = both[:, lead:]
    c_b[:, :lead] = both[:, :lead]
    sent.append(remote(p_send, p_recv, sem_ps.at[1], sem_pr.at[1], me, other))
    fb[0].wait()
    c_b[:, lead:gcol] = dot_nt(xb[...], w_b[...])
    lane = lax.broadcasted_iota(jnp.int32, (total_rows, acol), 1)
    mine = jnp.where(lane < gcol, c_b[:, :acol], p_send[...])
    arrived(sq_recv, sem_pr.at[0])
    mean_square = (sq_send[:, :1] + sq_recv[:, :1]) / D
    inv = lax.rsqrt(mean_square + epsilon)
    arrived(p_recv, sem_pr.at[1])
    tot[:, :acol] = (mine + p_recv[...]) * inv
    whole = tot[...]
    wide_lane = lax.broadcasted_iota(jnp.int32, whole.shape, 1)
    span = whole.shape[1]
    features = pltpu.roll(
        jnp.where(wide_lane < gcol, whole, 0.0), lax.rem(me * gcol, LANE), 1
    )
    low = pltpu.roll(whole, span - gcol, 1)[:, :LANE]
    low_lane = lax.broadcasted_iota(jnp.int32, low.shape, 1)
    low = pltpu.roll(jnp.where(low_lane < scol, low, 0.0), lax.rem(me * scol, LANE), 1)
    step_all = pltpu.roll(whole, span - gcol - scol, 1)[:, :LANE]
    step_f[...] = pltpu.roll(step_all, lax.rem(LANE - s * m_heads, LANE), 1)
    tot[...] = features
    c_b[:, :LANE] = low
    for r in range(n):
        f_send[r, :, :fpad] = tot[rows * r : rows * (r + 1), :].astype(BF16)
        f_send[r, :, fpad:] = c_b[rows * r : rows * (r + 1), :LANE].astype(BF16)
    for k in range(n - 1):
        to = far_first(k)
        remote(f_send.at[to], f_recv.at[me], sem_fs, sem_fr, to, s)
    own_f = pltpu.make_async_copy(f_send.at[me], f_recv.at[me], sem_loc.at[0])
    own_f.start()

    half = total_rows // n_short

    def gate_up(c):
        part = slice(fspans[c][0], fspans[c][0] + fspans[c][1])
        fgu[c][0].wait()
        both = [dot(xb[...], g_v[:, part])]
        fgu[c][1].wait()
        both.append(dot(xb[...], u_v[:, part]))
        for k in range(2):
            for i in range(n_short):
                gsc[k, i, :, part] = both[k][half * i : half * (i + 1)] * inv[half * i : half * (i + 1)]
        for k in range(2):
            gu_send[k, :, part] = gsc[k, other, :, part].astype(BF16)
        sent.append(
            remote(
                gu_send.at[:, :, cols(c)], gu_recv.at[:, :, cols(c)], sem_us.at[c], sem_ur.at[c], me, other
            )
        )

    def hidden(c):
        part = slice(fspans[c][0], fspans[c][0] + fspans[c][1])
        arrived(gu_recv.at[:, :, cols(c)], sem_ur.at[c])
        a = gsc[0, s, :, part] + gu_recv[0, :, part].astype(F32)
        b = gsc[1, s, :, part] + gu_recv[1, :, part].astype(F32)
        hbuf[s, :, part] = (silu(a) * b).astype(BF16)
        sent.append(
            remote(
                hbuf.at[s, :, cols(c)], hbuf.at[s, :, cols(c)], sem_hs.at[c], sem_hr.at[c], me, other
            )
        )

    def down_part(c):
        part = slice(fspans[c][0], fspans[c][0] + fspans[c][1])
        arrived(hbuf.at[other, :, cols(c)], sem_hr.at[c])
        fdn[c].wait()
        term = dot(hbuf[:, :, part].reshape(total_rows, fspans[c][1]), d_v[part, :])
        xf[...] = term if c == 0 else xf[...] + term

    early = max(1, n_chunk - 1)
    for c in range(early):
        gate_up(c)
        if c:
            hidden(c - 1)

    own_f.wait()
    arrived(f_recv.at[pl.ds(0, n - 1)], sem_fr)
    fwidth = feat.shape[1]
    for j in range(n):
        base = gcol * j // LANE * LANE
        w = min(fpad, fwidth - base)
        feat[:, base : base + w] += f_recv[j, :, :w].astype(F32)
        base = scol * j // LANE * LANE
        bc[:, base : base + LANE] += f_recv[j, :, fpad:].astype(F32)
    for copy in fkv:
        copy.wait()
    k_at = q_heads * HEAD_SIZE
    v_at = k_at + kv_heads * HEAD_SIZE
    x_at = v_at + kv_heads * HEAD_SIZE
    z_at = x_at + m_heads * MP

    def turn(v):
        return v * cos_t + jnp.concatenate([v[:, HEAD_SIZE // 2 :], v[:, : HEAD_SIZE // 2]], axis=1) * sin_t

    length = lengths[0]
    for kv in range(kv_heads):
        for i in range(rep):
            h = kv * rep + i
            qbuf[kv, rows * i : rows * (i + 1), :] = turn(feat[:, h * HEAD_SIZE : (h + 1) * HEAD_SIZE])
        knbuf[kv, :rows, :] = turn(feat[:, k_at + kv * HEAD_SIZE : k_at + (kv + 1) * HEAD_SIZE])
        vnbuf[kv, :rows, :] = feat[:, v_at + kv * HEAD_SIZE : v_at + (kv + 1) * HEAD_SIZE]
        head = slice(kv * HEAD_SIZE, (kv + 1) * HEAD_SIZE)
        query = qbuf[kv].astype(BF16)
        scale = HEAD_SIZE ** (-0.5)
        old = dot_nt(query, k_v[:, head]) * scale
        new = dot_nt(query, knbuf[kv].astype(BF16)) * scale
        slot = lax.broadcasted_iota(jnp.int32, old.shape, 1)
        old = jnp.where(slot < length, old, -1e30)
        token = lax.rem(lax.broadcasted_iota(jnp.int32, new.shape, 0), rows)
        fresh = lax.broadcasted_iota(jnp.int32, new.shape, 1)
        new = jnp.where(fresh <= token, new, -1e30)
        top = jnp.maximum(
            jnp.max(old, axis=1, keepdims=True), jnp.max(new, axis=1, keepdims=True)
        )
        old = jnp.exp(old - top)
        new = jnp.exp(new - top)
        den = jnp.sum(old, axis=1, keepdims=True) + jnp.sum(new, axis=1, keepdims=True)
        obuf[kv] = (
            dot(old.astype(BF16), v_v[:, head]) + dot(new.astype(BF16), vnbuf[kv].astype(BF16))
        ) / den
        for i in range(rep):
            h = kv * rep + i
            own[:, h * HEAD_SIZE : (h + 1) * HEAD_SIZE] = obuf[kv, rows * i : rows * (i + 1), :]

    write = silu(bc[:, :NS])
    read = silu(bc[:, NS:])
    rest = read
    for i in range(3):
        piece = rest.astype(BF16).astype(F32)
        cbuf[rows * i : rows * (i + 1), :] = piece
        rest = rest - piece
    rbuf[...] = dot_nt(cbuf[...].astype(BF16), s_v[...])
    carried = rbuf[:rows] + rbuf[rows : 2 * rows] + rbuf[2 * rows : 3 * rows]
    raw = step_f[pl.ds(rows * me, rows), :][:, :m_heads] + bias[...]
    step = jnp.maximum(raw, 0.0) + jnp.log1p(jnp.exp(-jnp.abs(raw)))
    run = [step[:1]]
    for t in range(1, rows):
        run.append(run[-1] + step[t : t + 1])
    age = jnp.concatenate(run, axis=0) * rate[...]
    kept = jnp.exp(-age)
    tid = lax.broadcasted_iota(jnp.int32, age.shape, 0)
    mix = []
    for u in range(rows):
        overlap = jnp.sum(read * write[u : u + 1], axis=1, keepdims=True)
        fade = jnp.exp(-jnp.maximum(age - age[u : u + 1], 0.0))
        mix.append(jnp.where(tid >= u, fade, 0.0) * step[u : u + 1] * overlap)
    skips = skip[...]
    for h in range(m_heads):
        hs = slice(h * MP, (h + 1) * MP)
        active = silu(feat[:, x_at + h * MP : x_at + (h + 1) * MP])
        y = kept[:, h : h + 1] * carried[:, hs] + skips[:, h : h + 1] * active
        for u in range(rows):
            y = y + mix[u][:, h : h + 1] * active[u : u + 1]
        y = y * silu(feat[:, z_at + h * MP : z_at + (h + 1) * MP])
        ms = jnp.mean(y * y, axis=1, keepdims=True)
        at = (q_heads + h) * MP
        own[:, at : at + MP] = y * lax.rsqrt(ms + epsilon) * mixer_gain[:, hs]

    window = opad + LANE
    for j in range(n):
        base = ocol * j // LANE * LANE
        off = ocol * j - base
        v = own[:, base : base + window]
        if off:
            v = jnp.concatenate([v[:, off:], v[:, :off]], axis=1)
        m_send[j] = v[:, :opad].astype(BF16)
    for k in range(n):
        to = far_first(k) if k < n - 1 else me
        for e in range(n_short):
            if k < n - 1 or e:
                remote(
                    m_send.at[to], m_recv.at[s * n + me], sem_ms, sem_mr, to, lax.rem(s + e, n_short)
                )
    own_m = pltpu.make_async_copy(m_send.at[me], m_recv.at[s * n + me], sem_loc.at[1])
    own_m.start()

    for c in range(early, n_chunk):
        gate_up(c)
        hidden(c - 1)
    for c in range(n_chunk):
        if c == max(0, n_chunk - 2):
            hidden(n_chunk - 1)
        down_part(c)
    own_m.wait()
    arrived(m_recv.at[pl.ds(0, n * n_short - 1)], sem_mr)
    for g in range(n_short):
        for j in range(n):
            lhs[g, rows * j : rows * (j + 1), :] = m_recv[g * n + j].astype(F32)
    for copy in fmo:
        copy.wait()
    def out_to(o, k):
        to = upward(k)
        part = pl.ds(*ospans[o])
        remote(o_send.at[to, :, part], o_recv.at[me, :, part], sem_os.at[o], sem_or.at[o], to, s)

    for o in range(n_oc):
        oc = slice(ospans[o][0], ospans[o][0] + ospans[o][1])
        acc = xf[:, oc]
        for g in range(n_short):
            acc = acc + dot(lhs[g].astype(BF16), m_v[g, :, oc])
        xf[:, oc] = acc
        for r in range(n):
            o_send[r, :, oc] = xf[rows * r : rows * (r + 1), oc].astype(BF16)
        out_to(o, 0)
        if o:
            for k in range(1, n - 1):
                out_to(o - 1, k)
    for k in range(1, n - 1):
        out_to(n_oc - 1, k)
    for o in range(n_oc):
        part = pl.ds(*ospans[o])
        oc = slice(ospans[o][0], ospans[o][0] + ospans[o][1])
        acc = xg[me, :, oc].astype(F32) + o_send[me, :, oc].astype(F32)
        arrived(o_recv.at[pl.ds(0, n - 1), :, part], sem_or.at[o])
        for d in range(1, n):
            acc = acc + o_recv[peer(d), :, oc].astype(F32)
        out[:, oc] = acc.astype(BF16)
    for copy in sent:
        copy.wait_send()
    arrived(xg.at[pl.ds(0, n - 1)], sem_gs)
    arrived(f_send.at[pl.ds(0, n - 1)], sem_fs)
    arrived(m_recv.at[pl.ds(0, n * n_short - 1)], sem_ms)
    for o in range(n_oc):
        arrived(o_send.at[pl.ds(0, n - 1), :, pl.ds(*ospans[o])], sem_os.at[o])


def round_up(v):
    return -(-v // LANE) * LANE


def dims_lead(gcol):
    return min(LANE, gcol - 16)


def xpad(gcol):
    return round_up(gcol + LANE - 1)


def spans_of(width, piece):
    return tuple((at, min(piece, width - at)) for at in range(0, width, piece))


def fused(*args):
    (tokens, norm_gain, mixer_in, shared_in, step_in, step_bias, decay_rate, skip_gain,
     cached_keys, cached_values, lengths, state_cache, mixer_gain, mixer_out,
     gate_weight, up_weight, down_weight) = args
    n = lax.axis_size("wide")
    n_short = lax.axis_size("short")
    rows, width = tokens.shape
    gcol = mixer_in.shape[2]
    scol = shared_in.shape[1]
    ncol = step_in.shape[1]
    ocol = mixer_out.shape[1]
    ffl = gate_weight.shape[1]
    fspans = spans_of(ffl, 1024)
    first = min(512, width)
    ospans = ((0, first),) + tuple((first + at, size) for at, size in spans_of(width - first, 1024))
    n_chunk = len(fspans)
    n_oc = len(ospans)
    m_heads = MH // n_short
    kv_heads = KEY_VALUE_HEADS // n_short
    total_rows = n * rows
    acol = gcol + scol + ncol
    fpad = xpad(gcol)
    opad = round_up(ocol)
    lead = dims_lead(gcol)
    features = n * gcol
    outs = n * ocol
    half = total_rows // n_short
    dims = (n, n_short, rows, width, gcol, scol, ncol, ocol, fspans, ospans)
    vm = pl.BlockSpec(memory_space=pltpu.VMEM)
    hb = pl.BlockSpec(memory_space=pl.ANY)
    V = pltpu.VMEM
    dma = pltpu.SemaphoreType.DMA
    kvw = cached_keys.shape[2]
    slots = cached_keys.shape[1]
    scratch = [
        V((width // LANE, LANE), F32), V((1, m_heads), F32), V((1, m_heads), F32),
        V((1, m_heads), F32), V((1, m_heads * MP), F32),
        V((lead + acol, width), BF16), V((gcol - lead, width), BF16), V((slots, kvw), BF16),
        V((slots, kvw), BF16), V((m_heads * MP, NS), BF16),
        V((width, ffl), BF16), V((width, ffl), BF16),
        V((n_short, opad, width), BF16), V((ffl, width), BF16),
        V((n, rows, width), BF16), V((total_rows, width), F32), V((total_rows, width), BF16),
        V((total_rows, LANE), F32), V((total_rows, LANE), F32),
        V((total_rows, acol), F32), V((total_rows, acol), F32), V((total_rows, fpad), F32),
        V((total_rows, fpad), F32), V((total_rows, LANE), F32),
        V((n, rows, fpad + LANE), BF16), V((n, rows, fpad + LANE), BF16),
        V((rows, features), F32), V((rows, 2 * NS), F32),
        V((kv_heads, 32, HEAD_SIZE), F32), V((kv_heads, 16, HEAD_SIZE), F32),
        V((kv_heads, 16, HEAD_SIZE), F32), V((kv_heads, 32, HEAD_SIZE), F32),
        V((16, NS), F32), V((16, m_heads * MP), F32),
        V((rows, round_up(outs) + opad + LANE), F32),
        V((n, rows, opad), BF16), V((n_short * n, rows, opad), BF16),
        V((n_short, total_rows, opad), F32),
        V((2, n_short, half, ffl), F32),
        V((2, half, ffl), BF16), V((2, half, ffl), BF16),
        V((n_short, half, ffl), BF16),
        V((n, rows, width), BF16), V((n, rows, width), BF16),
        dma((6 + 5 + 3 * n_chunk + 3 + n_short,)), dma((2,)),
        dma, dma, dma((2,)), dma((2,)), dma, dma,
        dma, dma, dma((n_chunk,)), dma((n_chunk,)),
        dma((n_chunk,)), dma((n_chunk,)), dma((n_oc,)), dma((n_oc,)),
    ]
    return pl.pallas_call(
        functools.partial(fused_kernel, dims),
        out_shape=pltpu.VMEM((rows, width), BF16),
        in_specs=[hb] * 5 + [pl.BlockSpec(memory_space=pltpu.SMEM)] + [hb] * 11,
        out_specs=vm,
        scratch_shapes=scratch,
        name="layer",
        compiler_params=pltpu.CompilerParams(
            collective_id=0, has_side_effects=True, vmem_limit_bytes=66 * 1000 * 1000
        ),
    )(
        tokens, norm_gain.reshape(width // LANE, LANE), step_bias[None, :], decay_rate[None, :],
        skip_gain[None, :], lengths, mixer_gain[None, :],
        jnp.transpose(mixer_in, (1, 2, 0)), shared_in.T, step_in.T,
        cached_keys[0], cached_values[0], state_cache.reshape(m_heads * MP, NS),
        mixer_out, gate_weight, up_weight, down_weight,
    )


def fits(n, n_short, args):
    tokens, mixer_in, shared_in, step_in = args[0], args[2], args[3], args[4]
    return (
        n_short == 2
        and tokens.shape[0] == DRAFT_TOKENS
        and n * DRAFT_TOKENS == 32
        and mixer_in.shape[2] % 16 == 0
        and shared_in.shape[1] % 16 == 0
        and LANE % shared_in.shape[1] == 0
        and step_in.shape[1] % 16 == 0
        and args[13].shape[1] % 16 == 0
        and args[14].shape[1] % LANE == 0
        and tokens.shape[1] % LANE == 0
    )


def layer(*args):
    if fits(lax.axis_size("wide"), lax.axis_size("short"), args):
        return fused(*args)
    return on_device(*args)


def solution(mesh):
    in_specs = (
        P(("groups", "wide"), "short"),
        P("short"),
        P("short", None, "wide"),
        P("short", "wide"),
        P("short", None),
        P("short"),
        P("short"),
        P("short"),
        P(("groups", "wide"), None, "short"),
        P(("groups", "wide"), None, "short"),
        P(("groups", "wide")),
        P(("groups", "wide"), "short", None, None),
        P("short"),
        P(None, "wide", "short"),
        P("short", "wide"),
        P("short", "wide"),
        P("wide", "short"),
    )
    out_specs = P(("groups", "wide"), "short")
    return jax.shard_map(
        layer, mesh=mesh, in_specs=in_specs, out_specs=out_specs, check_vma=False
    )
```

```python
import functools
import math
import jax
import jax.numpy as jnp
from jax import lax
from jax.experimental import pallas as pl
from jax.experimental.pallas import tpu as pltpu
from jax.sharding import PartitionSpec as P

D = 5120
QUERY_HEADS = 20
KEY_VALUE_HEADS = 4
HEAD_SIZE = 128
MH = 32
MP = 128
NS = 256
CACHE_SLOTS = 512
DRAFT_TOKENS = 4


epsilon = 1e-05


def as_sent(x):

    def short(part):
        return part.astype(jnp.bfloat16) if part.dtype == jnp.float32 else part

    return jax.tree.map(short, x)


def rotate(vectors, cos_table, sin_table):
    half_width = vectors.shape[-1] // 2
    first_half = vectors[..., :half_width]
    second_half = vectors[..., half_width:]
    return jnp.concatenate(
        [
            first_half * cos_table - second_half * sin_table,
            second_half * cos_table + first_half * sin_table,
        ],
        axis=-1,
    )


def rope_tables(positions):
    frequency = 10000.0 ** (-(jnp.arange(HEAD_SIZE // 2, dtype=jnp.float32) * 2.0 / HEAD_SIZE))
    angles = positions.astype(jnp.float32)[..., None] * frequency
    return (jnp.cos(angles), jnp.sin(angles))


def attend_one(queries, fresh_keys, fresh_values, key_tile_block, value_tile_block, length):
    score_scale = HEAD_SIZE ** (-0.5)
    scores_cache = (
        jnp.einsum("tkgd,pkd->kgtp", queries, key_tile_block, preferred_element_type=jnp.float32)
        * score_scale
    )
    scores_new = (
        jnp.einsum("tkgd,ukd->kgtu", queries, fresh_keys, preferred_element_type=jnp.float32)
        * score_scale
    )
    live_keys = jnp.arange(key_tile_block.shape[0], dtype=jnp.int32) < length
    causal = jnp.arange(DRAFT_TOKENS)[None, :] <= jnp.arange(DRAFT_TOKENS)[:, None]
    scores_cache = jnp.where(live_keys, scores_cache, -1e30)
    scores_new = jnp.where(causal, scores_new, -1e30)
    highest = jnp.maximum(jnp.max(scores_cache, axis=-1), jnp.max(scores_new, axis=-1))[..., None]
    weight_cache = jnp.exp(scores_cache - highest)
    weight_new = jnp.exp(scores_new - highest)
    denominator = jnp.sum(weight_cache, axis=-1, keepdims=True) + jnp.sum(
        weight_new, axis=-1, keepdims=True
    )
    probs_cache = (weight_cache / denominator).astype(jnp.bfloat16)
    probs_new = (weight_new / denominator).astype(jnp.bfloat16)
    attended = jnp.einsum(
        "kgtp,pkd->tkgd", probs_cache, value_tile_block, preferred_element_type=jnp.float32
    )
    attended = attended + jnp.einsum(
        "kgtu,ukd->tkgd", probs_new, fresh_values, preferred_element_type=jnp.float32
    )
    return attended.astype(jnp.bfloat16)


def scan_one(
    state_block, inputs_x, gates_z, b_vals, c_vals, step_sizes, decay_rates, skip_gain, head_gain
):
    hstate = state_block.astype(jnp.float32)
    in_active = jax.nn.silu(inputs_x.astype(jnp.float32))
    write_vec = jax.nn.silu(b_vals.astype(jnp.float32))
    read_vec = jax.nn.silu(c_vals.astype(jnp.float32))
    outputs = []
    for draft_index in range(DRAFT_TOKENS):
        decays = jnp.exp(-step_sizes[draft_index] * decay_rates)
        inject = (step_sizes[draft_index][:, None] * in_active[draft_index])[
            :, :, None
        ] * write_vec[draft_index][None, None, :]
        hstate = decays[:, None, None] * hstate + inject
        readout = jnp.einsum(
            "hpn,n->hp", hstate, read_vec[draft_index], precision=lax.Precision.HIGHEST
        )
        outputs.append(readout + skip_gain[:, None] * in_active[draft_index])
    gated = jnp.stack(outputs) * jax.nn.silu(gates_z.astype(jnp.float32))
    mean_square = jnp.mean(gated * gated, axis=-1, keepdims=True)
    return (gated * lax.rsqrt(mean_square + epsilon) * head_gain).astype(jnp.bfloat16)


def on_device(
    tokens,
    norm_gain,
    mixer_in,
    shared_in,
    step_in,
    step_bias,
    decay_rate,
    skip_gain,
    cached_keys,
    cached_values,
    lengths,
    state_cache,
    mixer_gain,
    mixer_out,
    gate_weight,
    up_weight,
    down_weight,
):
    short_count = lax.axis_size("short")
    n_wide = lax.axis_size("wide")
    q_heads = QUERY_HEADS // short_count
    key_value_heads = KEY_VALUE_HEADS // short_count
    ssm_heads = MH // short_count
    repeat_factor = QUERY_HEADS // KEY_VALUE_HEADS
    query_size = q_heads * HEAD_SIZE
    key_size = key_value_heads * HEAD_SIZE
    m_size = ssm_heads * MP
    local_rows = tokens.shape[0]
    requests = local_rows // DRAFT_TOKENS
    width_half = tokens.shape[1]
    rows_float = tokens.astype(jnp.float32)
    square_sum = lax.psum(jnp.sum(rows_float * rows_float, axis=1), "short")
    inv_rms = lax.rsqrt(square_sum / D + epsilon)
    normed = (rows_float * inv_rms[:, None] * norm_gain[None, :]).astype(jnp.bfloat16)
    step_terms = jnp.dot(normed, step_in, preferred_element_type=jnp.float32)
    step_raw = lax.psum_scatter(step_terms, "short", scatter_dimension=1, tiled=True)
    gathered = lax.all_gather(normed, "wide", axis=0, tiled=True)
    group_part = jnp.einsum("rd,dgc->rgc", gathered, mixer_in, preferred_element_type=jnp.float32)
    shared_part = jnp.dot(gathered, shared_in, preferred_element_type=jnp.float32)[:, None, :]
    gate_part = jnp.dot(gathered, gate_weight, preferred_element_type=jnp.float32)
    up_part = jnp.dot(gathered, up_weight, preferred_element_type=jnp.float32)
    gate_half, up_half = (
        lax.psum_scatter(
            gate_part.astype(jnp.bfloat16), "short", scatter_dimension=0, tiled=True
        ).astype(jnp.float32),
        lax.psum_scatter(
            up_part.astype(jnp.bfloat16), "short", scatter_dimension=0, tiled=True
        ).astype(jnp.float32),
    )
    hidden_half = (jax.nn.silu(gate_half) * up_half).astype(jnp.bfloat16)
    hidden = lax.all_gather(hidden_half, "short", axis=0, tiled=True)
    group_moved, shared_moved = (
        lax.all_to_all(group_part, "wide", split_axis=0, concat_axis=2, tiled=True),
        lax.all_to_all(shared_part, "wide", split_axis=0, concat_axis=2, tiled=True),
    )
    group_sum = lax.psum_scatter(group_moved, "short", scatter_dimension=1, tiled=True)
    shared_sum = lax.psum(shared_moved, "short")
    features = group_sum[:, 0, :].astype(jnp.bfloat16)
    shared_vals = shared_sum[:, 0, :].astype(jnp.bfloat16)
    queries = features[:, :query_size].reshape(requests, DRAFT_TOKENS, q_heads, HEAD_SIZE)
    fresh_keys = features[:, query_size : query_size + key_size].reshape(
        requests, DRAFT_TOKENS, key_value_heads, HEAD_SIZE
    )
    fresh_values = features[:, query_size + key_size : query_size + 2 * key_size].reshape(
        requests, DRAFT_TOKENS, key_value_heads, HEAD_SIZE
    )
    x_start = query_size + 2 * key_size
    inputs_x = features[:, x_start : x_start + m_size].reshape(
        requests, DRAFT_TOKENS, ssm_heads, MP
    )
    gates_z = features[:, x_start + m_size : x_start + 2 * m_size].reshape(
        requests, DRAFT_TOKENS, ssm_heads, MP
    )
    positions = lengths[:, None] + jnp.arange(DRAFT_TOKENS, dtype=jnp.int32)[None, :]
    cos_table, sin_table = rope_tables(positions)
    cos_table = cos_table[:, :, None, :]
    sin_table = sin_table[:, :, None, :]
    rotated_queries = rotate(queries.astype(jnp.float32), cos_table, sin_table).astype(jnp.bfloat16)
    keys_rot = rotate(fresh_keys.astype(jnp.float32), cos_table, sin_table).astype(jnp.bfloat16)
    rotated_queries = rotated_queries.reshape(
        requests, DRAFT_TOKENS, key_value_heads, repeat_factor, HEAD_SIZE
    )
    key_tile_block = cached_keys.reshape(requests, CACHE_SLOTS, key_value_heads, HEAD_SIZE)
    value_tile_block = cached_values.reshape(requests, CACHE_SLOTS, key_value_heads, HEAD_SIZE)
    attention = jax.vmap(attend_one)(
        rotated_queries, keys_rot, fresh_values, key_tile_block, value_tile_block, lengths
    )
    step_sizes = jax.nn.softplus(
        step_raw.reshape(requests, DRAFT_TOKENS, ssm_heads) + step_bias[None, None, :]
    )
    b_vals = shared_vals[:, :NS].reshape(requests, DRAFT_TOKENS, NS)
    c_vals = shared_vals[:, NS:].reshape(requests, DRAFT_TOKENS, NS)
    head_gain = mixer_gain.reshape(ssm_heads, MP)
    mamba = jax.vmap(scan_one, in_axes=(0, 0, 0, 0, 0, 0, None, None, None))(
        state_cache, inputs_x, gates_z, b_vals, c_vals, step_sizes, decay_rate, skip_gain, head_gain
    )
    own_rows = jnp.concatenate(
        [attention.reshape(local_rows, query_size), mamba.reshape(local_rows, m_size)], axis=1
    )
    returned = lax.all_to_all(
        as_sent(own_rows[:, None, :]), "wide", split_axis=2, concat_axis=0, tiled=True
    )
    both_groups = lax.all_gather(as_sent(returned), "short", axis=1, tiled=True).astype(
        returned.dtype
    )
    projected = jnp.einsum(
        "rgc,gcd->rd", both_groups, mixer_out, preferred_element_type=jnp.float32
    )
    summed = projected + jnp.dot(hidden, down_weight, preferred_element_type=jnp.float32)
    pieces = lax.all_to_all(
        summed.reshape(n_wide, local_rows, width_half).astype(jnp.bfloat16),
        "wide",
        split_axis=0,
        concat_axis=0,
        tiled=True,
    ).astype(jnp.float32)
    total = rows_float + jnp.sum(pieces, axis=0)
    return total.astype(jnp.bfloat16)


MESH = pl.DeviceIdType.MESH
F32 = jnp.float32
BF16 = jnp.bfloat16
NT = (((1,), (1,)), ((), ()))
LANE = 128


def silu(v):
    return v / (1.0 + jnp.exp(-v))


def dot(a, b):
    return jnp.dot(a, b, preferred_element_type=F32)


def dot_nt(a, b):
    return lax.dot_general(a, b, NT, preferred_element_type=F32)


def rope_rows(length, rows):
    lane = lax.broadcasted_iota(jnp.int32, (rows, HEAD_SIZE), 1)
    token = lax.broadcasted_iota(jnp.int32, (rows, HEAD_SIZE), 0)
    pair = lax.rem(lane, HEAD_SIZE // 2).astype(F32)
    angle = (token + length).astype(F32) * jnp.exp(pair * (-2.0 * math.log(10000.0) / HEAD_SIZE))
    turns = jnp.floor(angle * (2.0 / math.pi) + 0.5)
    rest = angle - turns * 1.5703125
    rest = rest - turns * 4.837512969970703125e-4
    rest = rest - turns * 7.54978995489188216e-8
    z = rest * rest
    sine = ((-1.9515295891e-4 * z + 8.3321608736e-3) * z - 1.6666654611e-1) * z * rest + rest
    cosine = (2.443315711809948e-5 * z - 1.388731625493765e-3) * z + 4.166664568298827e-2
    cosine = cosine * z * z - 0.5 * z + 1.0
    quarter = turns - 4.0 * jnp.floor(turns * 0.25)
    odd = (quarter == 1.0) | (quarter == 3.0)
    cos_t = jnp.where(odd, sine, cosine)
    cos_t = jnp.where((quarter == 1.0) | (quarter == 2.0), -cos_t, cos_t)
    sin_t = jnp.where(odd, cosine, sine)
    sin_t = jnp.where(quarter >= 2.0, -sin_t, sin_t)
    return cos_t, jnp.where(lane < HEAD_SIZE // 2, -sin_t, sin_t)


def fused_kernel(
    dims,
    tokens, gain_h, bias_h, rate_h, skip_h, lengths, mixer_gain_h,
    mixer_in, shared_in, step_in, keys, values, state, mixer_out, gate, up, down,
    out,
    gain, bias, rate, skip, mixer_gain,
    w_a, w_b, k_v, v_v, s_v, g_v, u_v, m_v, d_v,
    xg, xf, xb, p_send, p_recv, c_b, tot, step_f,
    f_send, f_recv, feat, bc, qbuf, knbuf, vnbuf, obuf, cbuf, rbuf, own,
    m_send, m_recv, lhs, lhs_b, gsc, gu_send, gu_recv, hbuf, o_send, o_recv,
    sem_w, sem_loc, sem_r, sem_gs, sem_gr, sem_ps, sem_pr, sem_fs, sem_fr,
    sem_ms, sem_mr, sem_us, sem_ur, sem_hs, sem_hr, sem_os, sem_or,
):
    n, n_short, rows, width, gcol, scol, ncol, ocol, fspans, ospans = dims
    n_chunk = len(fspans)
    n_oc = len(ospans)
    total_rows = n * rows
    me = lax.axis_index("wide")
    s = lax.axis_index("short")
    other = 1 - s
    q_heads = QUERY_HEADS // n_short
    kv_heads = KEY_VALUE_HEADS // n_short
    m_heads = MH // n_short
    rep = QUERY_HEADS // KEY_VALUE_HEADS
    acol = gcol + scol + ncol
    sq_width = round_up(acol + 1) - acol
    fpad = xpad(gcol)
    opad = round_up(ocol + ocol % LANE)

    def peer(d):
        return lax.rem(me + d, n)

    def upward(k):
        return jnp.where(me <= k, k + 1, k)

    def far_first(k):
        down_to = n - 1 - k
        return jnp.where(2 * me >= n, upward(k), jnp.where(down_to > me, down_to, down_to - 1))

    weights = []

    def fetch(src, dst):
        copy = pltpu.make_async_copy(src, dst, sem_w.at[len(weights)])
        copy.start()
        weights.append(copy)
        return copy

    late = n // 2
    early = me < late

    def tell(sem, wide, short):
        pl.semaphore_signal(
            sem, inc=1, device_id={"wide": wide, "short": short}, device_id_type=MESH
        )

    barrier = pltpu.get_barrier_semaphore()
    for k in range(late):
        to = n - 1 - k

        @pl.when(me != to)
        def _(to=to):
            tell(barrier, to, s)

    @pl.when(early)
    def _():
        for k in range(1, late):
            tell(barrier, lax.rem(me + k, late), s)

    tell(barrier, me, other)

    own_tokens = fetch(tokens, xg.at[me])
    small = [
        fetch(gain_h, gain), fetch(bias_h, bias), fetch(rate_h, rate), fetch(skip_h, skip),
        fetch(mixer_gain_h, mixer_gain),
    ]
    lead = dims_lead(gcol)
    sem_a = len(weights)
    for src, dst in (
        (mixer_in.at[s, pl.ds(0, lead)], w_a.at[pl.ds(0, lead)]),
        (mixer_in.at[other], w_a.at[pl.ds(lead, gcol)]),
        (shared_in, w_a.at[pl.ds(lead + gcol, scol)]),
        (step_in, w_a.at[pl.ds(lead + gcol + scol, ncol)]),
    ):
        pltpu.make_async_copy(src, dst, sem_w.at[sem_a]).start()
    weights.append(None)
    fb = [fetch(mixer_in.at[s, pl.ds(lead, gcol - lead)], w_b)]

    def cols(c):
        return pl.ds(*fspans[c])

    fgu = []
    for c in range(n_chunk):
        fgu.append(
            (fetch(gate.at[:, cols(c)], g_v.at[:, cols(c)]), fetch(up.at[:, cols(c)], u_v.at[:, cols(c)]))
        )
        if c == 0:
            fkv = [fetch(keys, k_v), fetch(values, v_v), fetch(state, s_v)]
    fdn = [fetch(down.at[cols(c)], d_v.at[cols(c)]) for c in range(n_chunk)]
    sem_m = len(weights)
    for g in range(n_short):
        pltpu.make_async_copy(
            mixer_out.at[g], m_v.at[pl.ds(g * ocol, ocol)], sem_w.at[sem_m]
        ).start()

    def remote(src, dst, send, recv, wide, short):
        copy = pltpu.make_async_remote_copy(
            src_ref=src, dst_ref=dst, send_sem=send, recv_sem=recv,
            device_id={"wide": wide, "short": short}, device_id_type=MESH,
        )
        copy.start()
        return copy

    def arrived(buf, recv):
        pltpu.make_async_copy(buf, buf, recv).wait()

    sent = []

    def give(wide):
        remote(tokens, xg.at[me], sem_gs, sem_gr, wide, s)

    pl.semaphore_wait(barrier, jnp.where(early, late, n))

    @pl.when(early)
    def _():
        for k in range(1, late):
            give(lax.rem(me + k, late))
        pl.semaphore_wait(sem_r, 1)
        for k in range(late):
            give(n - 1 - k)

    @pl.when(me >= late)
    def _():
        tell(sem_r, jnp.where(me >= n - 2, me - (n - 2), me - 2), s)
        for k in range(late):
            give(k)
        for k in range(1, late):
            give(late + lax.rem(me + k, late))

    feat[...] = jnp.zeros_like(feat)
    bc[...] = jnp.zeros_like(bc)
    qbuf[...] = jnp.zeros_like(qbuf)
    knbuf[...] = jnp.zeros_like(knbuf)
    vnbuf[...] = jnp.zeros_like(vnbuf)
    cbuf[...] = jnp.zeros_like(cbuf)
    c_b[...] = jnp.zeros_like(c_b)
    tot[...] = jnp.zeros_like(tot)
    own[...] = jnp.zeros_like(own)
    for copy in small:
        copy.wait()
    cos_t, sin_t = rope_rows(lengths[0], rows)
    own_tokens.wait()
    arrived(xg.at[pl.ds(0, n - 1)], sem_gr)
    for j in range(n):
        xf[rows * j : rows * (j + 1), :] = xg[j].astype(F32)
    x = xf[...]
    squares = jnp.sum(x * x, axis=1, keepdims=True)
    p_send[:, acol:] = jnp.broadcast_to(squares, (total_rows, sq_width))
    for j in range(width // LANE):
        lanes = slice(j * LANE, (j + 1) * LANE)
        xb[:, lanes] = (xf[:, lanes] * gain[j : j + 1, :]).astype(BF16)

    arrived(w_a, sem_w.at[sem_a])
    both = dot_nt(xb[...], w_a[...])
    p_send[:, :acol] = both[:, lead:]
    c_b[:, :lead] = both[:, :lead]
    sent.append(remote(p_send, p_recv, sem_ps, sem_pr, me, other))
    fb[0].wait()
    c_b[:, lead:gcol] = dot_nt(xb[...], w_b[...])
    lane = lax.broadcasted_iota(jnp.int32, (total_rows, acol), 1)
    mine = jnp.where(lane < gcol, c_b[:, :acol], p_send[:, :acol])
    arrived(p_recv, sem_pr)
    mean_square = (squares + p_recv[:, acol : acol + 1]) / D
    inv = lax.rsqrt(mean_square + epsilon)
    tot[:, :acol] = (mine + p_recv[:, :acol]) * inv
    whole = tot[...]
    wide_lane = lax.broadcasted_iota(jnp.int32, whole.shape, 1)
    span = whole.shape[1]
    features = pltpu.roll(
        jnp.where(wide_lane < gcol, whole, 0.0), lax.rem(me * gcol, LANE), 1
    )
    low = pltpu.roll(whole, span - gcol, 1)[:, :LANE]
    low_lane = lax.broadcasted_iota(jnp.int32, low.shape, 1)
    low = pltpu.roll(jnp.where(low_lane < scol, low, 0.0), lax.rem(me * scol, LANE), 1)
    step_all = pltpu.roll(whole, span - gcol - scol, 1)[:, :LANE]
    step_f[...] = pltpu.roll(step_all, lax.rem(LANE - s * m_heads, LANE), 1)
    tot[...] = features
    c_b[:, :LANE] = low
    for r in range(n):
        f_send[r, :, :fpad] = tot[rows * r : rows * (r + 1), :].astype(BF16)
        f_send[r, :, fpad:] = c_b[rows * r : rows * (r + 1), :LANE].astype(BF16)
    for k in range(n - 1):
        to = far_first(k)
        remote(f_send.at[to], f_recv.at[me], sem_fs, sem_fr, to, s)
    own_f = pltpu.make_async_copy(f_send.at[me], f_recv.at[me], sem_loc.at[0])
    own_f.start()

    half = total_rows // n_short

    def gate_up(c):
        part = slice(fspans[c][0], fspans[c][0] + fspans[c][1])
        fgu[c][0].wait()
        fgu[c][1].wait()
        both = [dot(xb[...], g_v[:, part]), dot(xb[...], u_v[:, part])]
        for k in range(2):
            for i in range(n_short):
                gsc[k, i, :, part] = both[k][half * i : half * (i + 1)] * inv[half * i : half * (i + 1)]
        for k in range(2):
            gu_send[k, :, part] = gsc[k, other, :, part].astype(BF16)
        sent.append(
            remote(
                gu_send.at[:, :, cols(c)], gu_recv.at[:, :, cols(c)], sem_us.at[c], sem_ur.at[c], me, other
            )
        )

    def hidden(c):
        part = slice(fspans[c][0], fspans[c][0] + fspans[c][1])
        arrived(gu_recv.at[:, :, cols(c)], sem_ur.at[c])
        a = gsc[0, s, :, part] + gu_recv[0, :, part].astype(F32)
        b = gsc[1, s, :, part] + gu_recv[1, :, part].astype(F32)
        hbuf[s, :, part] = (silu(a) * b).astype(BF16)
        sent.append(
            remote(
                hbuf.at[s, :, cols(c)], hbuf.at[s, :, cols(c)], sem_hs.at[c], sem_hr.at[c], me, other
            )
        )

    def down_part(at, size):
        part = slice(at, at + size)
        term = dot(hbuf[:, :, part].reshape(total_rows, size), d_v[part, :])
        xf[...] = term if at == 0 else xf[...] + term

    def hidden_in(c):
        arrived(hbuf.at[other, :, cols(c)], sem_hr.at[c])
        fdn[c].wait()

    gate_up(0)

    own_f.wait()
    arrived(f_recv.at[pl.ds(0, n - 1)], sem_fr)
    fwidth = feat.shape[1]
    for j in range(n):
        base = gcol * j // LANE * LANE
        w = min(fpad, fwidth - base)
        feat[:, base : base + w] += f_recv[j, :, :w].astype(F32)
        base = scol * j // LANE * LANE
        bc[:, base : base + LANE] += f_recv[j, :, fpad:].astype(F32)
    for copy in fkv:
        copy.wait()
    k_at = q_heads * HEAD_SIZE
    v_at = k_at + kv_heads * HEAD_SIZE
    x_at = v_at + kv_heads * HEAD_SIZE
    z_at = x_at + m_heads * MP

    def turn(v):
        return v * cos_t + jnp.concatenate([v[:, HEAD_SIZE // 2 :], v[:, : HEAD_SIZE // 2]], axis=1) * sin_t

    length = lengths[0]
    for kv in range(kv_heads):
        for i in range(rep):
            h = kv * rep + i
            qbuf[kv, rows * i : rows * (i + 1), :] = turn(feat[:, h * HEAD_SIZE : (h + 1) * HEAD_SIZE])
        knbuf[kv, :rows, :] = turn(feat[:, k_at + kv * HEAD_SIZE : k_at + (kv + 1) * HEAD_SIZE])
        vnbuf[kv, :rows, :] = feat[:, v_at + kv * HEAD_SIZE : v_at + (kv + 1) * HEAD_SIZE]
        head = slice(kv * HEAD_SIZE, (kv + 1) * HEAD_SIZE)
        query = qbuf[kv].astype(BF16)
        scale = HEAD_SIZE ** (-0.5)
        old = dot_nt(query, k_v[:, head]) * scale
        new = dot_nt(query, knbuf[kv].astype(BF16)) * scale
        slot = lax.broadcasted_iota(jnp.int32, old.shape, 1)
        old = jnp.where(slot < length, old, -1e30)
        token = lax.rem(lax.broadcasted_iota(jnp.int32, new.shape, 0), rows)
        fresh = lax.broadcasted_iota(jnp.int32, new.shape, 1)
        new = jnp.where(fresh <= token, new, -1e30)
        top = jnp.maximum(
            jnp.max(old, axis=1, keepdims=True), jnp.max(new, axis=1, keepdims=True)
        )
        old = jnp.exp(old - top)
        new = jnp.exp(new - top)
        den = jnp.sum(old, axis=1, keepdims=True) + jnp.sum(new, axis=1, keepdims=True)
        obuf[kv] = (
            dot(old.astype(BF16), v_v[:, head]) + dot(new.astype(BF16), vnbuf[kv].astype(BF16))
        ) / den
        for i in range(rep):
            h = kv * rep + i
            own[:, h * HEAD_SIZE : (h + 1) * HEAD_SIZE] = obuf[kv, rows * i : rows * (i + 1), :]

    write = silu(bc[:, :NS])
    read = silu(bc[:, NS:])
    rest = read
    for i in range(3):
        piece = rest.astype(BF16).astype(F32)
        cbuf[rows * i : rows * (i + 1), :] = piece
        rest = rest - piece
    rbuf[...] = dot_nt(cbuf[...].astype(BF16), s_v[...])
    carried = rbuf[:rows] + rbuf[rows : 2 * rows] + rbuf[2 * rows : 3 * rows]
    raw = step_f[pl.ds(rows * me, rows), :][:, :m_heads] + bias[...]
    step = jnp.maximum(raw, 0.0) + jnp.log1p(jnp.exp(-jnp.abs(raw)))
    run = [step[:1]]
    for t in range(1, rows):
        run.append(run[-1] + step[t : t + 1])
    age = jnp.concatenate(run, axis=0) * rate[...]
    kept = jnp.exp(-age)
    tid = lax.broadcasted_iota(jnp.int32, age.shape, 0)
    mix = []
    for u in range(rows):
        overlap = jnp.sum(read * write[u : u + 1], axis=1, keepdims=True)
        fade = jnp.exp(-jnp.maximum(age - age[u : u + 1], 0.0))
        mix.append(jnp.where(tid >= u, fade, 0.0) * step[u : u + 1] * overlap)
    skips = skip[...]
    for h in range(m_heads):
        hs = slice(h * MP, (h + 1) * MP)
        active = silu(feat[:, x_at + h * MP : x_at + (h + 1) * MP])
        y = kept[:, h : h + 1] * carried[:, hs] + skips[:, h : h + 1] * active
        for u in range(rows):
            y = y + mix[u][:, h : h + 1] * active[u : u + 1]
        y = y * silu(feat[:, z_at + h * MP : z_at + (h + 1) * MP])
        ms = jnp.mean(y * y, axis=1, keepdims=True)
        at = (q_heads + h) * MP
        own[:, at : at + MP] = y * lax.rsqrt(ms + epsilon) * mixer_gain[:, hs]

    window = opad + LANE
    for j in range(n):
        base = ocol * j // LANE * LANE
        off = ocol * j - base
        v = own[:, base : base + window]
        if off:
            v = jnp.concatenate([v[:, off:], v[:, :off]], axis=1)
        m_send[j] = v[:, :opad].astype(BF16)
    for k in range(n):
        to = far_first(k) if k < n - 1 else me
        for e in range(n_short):
            if k < n - 1 or e:
                remote(
                    m_send.at[to], m_recv.at[s * n + me], sem_ms, sem_mr, to, lax.rem(s + e, n_short)
                )
    own_m = pltpu.make_async_copy(m_send.at[me], m_recv.at[s * n + me], sem_loc.at[1])
    own_m.start()

    hidden(0)
    for c in range(1, n_chunk):
        gate_up(c)
    hidden_in(0)
    pieces = spans_of(fspans[0][1], 1024)
    for k, (at, size) in enumerate(pieces):
        if k == len(pieces) - 1:
            for c in range(1, n_chunk):
                hidden(c)
        down_part(at, size)
    for c in range(1, n_chunk):
        hidden_in(c)
        down_part(*fspans[c])
    own_m.wait()
    arrived(m_recv.at[pl.ds(0, n * n_short - 1)], sem_mr)
    for g in range(n_short):
        for j in range(n):
            lhs[g, rows * j : rows * (j + 1), :] = m_recv[g * n + j].astype(F32)
    shift = ocol % LANE
    at = ocol - shift
    block_lane = lax.broadcasted_iota(jnp.int32, (total_rows, opad), 1)
    first = jnp.where(block_lane < ocol, lhs[0], 0.0)
    second = pltpu.roll(lhs[1], shift, 1) if shift else lhs[1]
    second = jnp.where((block_lane >= shift) & (block_lane < shift + ocol), second, 0.0)
    lhs_b[:, :at] = first[:, :at].astype(BF16)
    lhs_b[:, at:opad] = (first[:, at:] + second[:, : opad - at]).astype(BF16)
    lhs_b[:, opad:] = second[:, opad - at :].astype(BF16)
    arrived(m_v, sem_w.at[sem_m])
    def out_to(o, k):
        to = upward(k)
        part = pl.ds(*ospans[o])
        remote(o_send.at[to, :, part], o_recv.at[me, :, part], sem_os.at[o], sem_or.at[o], to, s)

    for o in range(n_oc):
        oc = slice(ospans[o][0], ospans[o][0] + ospans[o][1])
        acc = xf[:, oc] + dot(lhs_b[:, : n_short * ocol], m_v[:, oc])
        xf[:, oc] = acc
        for r in range(n):
            o_send[r, :, oc] = xf[rows * r : rows * (r + 1), oc].astype(BF16)
        out_to(o, 0)
        if o:
            for k in range(1, n - 1):
                out_to(o - 1, k)
    for k in range(1, n - 1):
        out_to(n_oc - 1, k)
    for o in range(n_oc):
        part = pl.ds(*ospans[o])
        oc = slice(ospans[o][0], ospans[o][0] + ospans[o][1])
        acc = xg[me, :, oc].astype(F32) + o_send[me, :, oc].astype(F32)
        arrived(o_recv.at[pl.ds(0, n - 1), :, part], sem_or.at[o])
        for d in range(1, n):
            acc = acc + o_recv[peer(d), :, oc].astype(F32)
        out[:, oc] = acc.astype(BF16)
    for copy in sent:
        copy.wait_send()
    arrived(xg.at[pl.ds(0, n - 1)], sem_gs)
    arrived(f_send.at[pl.ds(0, n - 1)], sem_fs)
    arrived(m_recv.at[pl.ds(0, n * n_short - 1)], sem_ms)
    for o in range(n_oc):
        arrived(o_send.at[pl.ds(0, n - 1), :, pl.ds(*ospans[o])], sem_os.at[o])


def round_up(v):
    return -(-v // LANE) * LANE


def dims_lead(gcol):
    return min(LANE, gcol - 16)


def xpad(gcol):
    return round_up(gcol + LANE - 1)


def spans_of(width, piece):
    return tuple((at, min(piece, width - at)) for at in range(0, width, piece))


def fused(*args):
    (tokens, norm_gain, mixer_in, shared_in, step_in, step_bias, decay_rate, skip_gain,
     cached_keys, cached_values, lengths, state_cache, mixer_gain, mixer_out,
     gate_weight, up_weight, down_weight) = args
    n = lax.axis_size("wide")
    n_short = lax.axis_size("short")
    rows, width = tokens.shape
    gcol = mixer_in.shape[2]
    scol = shared_in.shape[1]
    ncol = step_in.shape[1]
    ocol = mixer_out.shape[1]
    ffl = gate_weight.shape[1]
    fspans = spans_of(ffl, 2048)
    first = min(1024, width)
    ospans = ((0, first),) + tuple((first + at, size) for at, size in spans_of(width - first, 1536))
    n_chunk = len(fspans)
    n_oc = len(ospans)
    m_heads = MH // n_short
    kv_heads = KEY_VALUE_HEADS // n_short
    total_rows = n * rows
    acol = gcol + scol + ncol
    sq_width = round_up(acol + 1) - acol
    fpad = xpad(gcol)
    opad = round_up(ocol + ocol % LANE)
    lead = dims_lead(gcol)
    features = n * gcol
    outs = n * ocol
    half = total_rows // n_short
    dims = (n, n_short, rows, width, gcol, scol, ncol, ocol, fspans, ospans)
    vm = pl.BlockSpec(memory_space=pltpu.VMEM)
    hb = pl.BlockSpec(memory_space=pl.ANY)
    V = pltpu.VMEM
    dma = pltpu.SemaphoreType.DMA
    kvw = cached_keys.shape[2]
    slots = cached_keys.shape[1]
    scratch = [
        V((width // LANE, LANE), F32), V((1, m_heads), F32), V((1, m_heads), F32),
        V((1, m_heads), F32), V((1, m_heads * MP), F32),
        V((lead + acol, width), BF16), V((gcol - lead, width), BF16), V((slots, kvw), BF16),
        V((slots, kvw), BF16), V((m_heads * MP, NS), BF16),
        V((width, ffl), BF16), V((width, ffl), BF16),
        V((n_short * ocol, width), BF16), V((ffl, width), BF16),
        V((n, rows, width), BF16), V((total_rows, width), F32), V((total_rows, width), BF16),
        V((total_rows, acol + sq_width), F32), V((total_rows, acol + sq_width), F32),
        V((total_rows, fpad), F32),
        V((total_rows, fpad), F32), V((total_rows, LANE), F32),
        V((n, rows, fpad + LANE), BF16), V((n, rows, fpad + LANE), BF16),
        V((rows, features), F32), V((rows, 2 * NS), F32),
        V((kv_heads, 32, HEAD_SIZE), F32), V((kv_heads, 16, HEAD_SIZE), F32),
        V((kv_heads, 16, HEAD_SIZE), F32), V((kv_heads, 32, HEAD_SIZE), F32),
        V((16, NS), F32), V((16, m_heads * MP), F32),
        V((rows, round_up(outs) + opad + LANE), F32),
        V((n, rows, opad), BF16), V((n_short * n, rows, opad), BF16),
        V((n_short, total_rows, opad), F32), V((total_rows, ocol // LANE * LANE + opad), BF16),
        V((2, n_short, half, ffl), F32),
        V((2, half, ffl), BF16), V((2, half, ffl), BF16),
        V((n_short, half, ffl), BF16),
        V((n, rows, width), BF16), V((n, rows, width), BF16),
        dma((6 + 2 + 3 * n_chunk + 3 + 1,)), dma((2,)),
        pltpu.SemaphoreType.REGULAR, dma, dma, dma, dma, dma, dma,
        dma, dma, dma((n_chunk,)), dma((n_chunk,)),
        dma((n_chunk,)), dma((n_chunk,)), dma((n_oc,)), dma((n_oc,)),
    ]
    return pl.pallas_call(
        functools.partial(fused_kernel, dims),
        out_shape=pltpu.VMEM((rows, width), BF16),
        in_specs=[hb] * 5 + [pl.BlockSpec(memory_space=pltpu.SMEM)] + [hb] * 11,
        out_specs=vm,
        scratch_shapes=scratch,
        name="layer",
        compiler_params=pltpu.CompilerParams(
            collective_id=0, has_side_effects=True, vmem_limit_bytes=66 * 1000 * 1000
        ),
    )(
        tokens, norm_gain.reshape(width // LANE, LANE), step_bias[None, :], decay_rate[None, :],
        skip_gain[None, :], lengths, mixer_gain[None, :],
        jnp.transpose(mixer_in, (1, 2, 0)), shared_in.T, step_in.T,
        cached_keys[0], cached_values[0], state_cache.reshape(m_heads * MP, NS),
        mixer_out, gate_weight, up_weight, down_weight,
    )


def fits(n, n_short, args):
    tokens, mixer_in, shared_in, step_in = args[0], args[2], args[3], args[4]
    return (
        n_short == 2
        and tokens.shape[0] == DRAFT_TOKENS
        and n * DRAFT_TOKENS == 32
        and mixer_in.shape[2] % 16 == 0
        and shared_in.shape[1] % 16 == 0
        and LANE % shared_in.shape[1] == 0
        and step_in.shape[1] % 16 == 0
        and args[13].shape[1] % 16 == 0
        and args[13].shape[1] >= LANE
        and args[14].shape[1] % LANE == 0
        and tokens.shape[1] % LANE == 0
    )


def layer(*args):
    if fits(lax.axis_size("wide"), lax.axis_size("short"), args):
        return fused(*args)
    return on_device(*args)


def solution(mesh):
    in_specs = (
        P(("groups", "wide"), "short"),
        P("short"),
        P("short", None, "wide"),
        P("short", "wide"),
        P("short", None),
        P("short"),
        P("short"),
        P("short"),
        P(("groups", "wide"), None, "short"),
        P(("groups", "wide"), None, "short"),
        P(("groups", "wide")),
        P(("groups", "wide"), "short", None, None),
        P("short"),
        P(None, "wide", "short"),
        P("short", "wide"),
        P("short", "wide"),
        P("wide", "short"),
    )
    out_specs = P(("groups", "wide"), "short")
    return jax.shard_map(
        layer, mesh=mesh, in_specs=in_specs, out_specs=out_specs, check_vma=False
    )
```

```python
import functools
import math
import jax
import jax.numpy as jnp
from jax import lax
from jax.experimental import pallas as pl
from jax.experimental.pallas import tpu as pltpu
from jax.sharding import PartitionSpec as P

D = 5120
QUERY_HEADS = 20
KEY_VALUE_HEADS = 4
HEAD_SIZE = 128
MH = 32
MP = 128
NS = 256
CACHE_SLOTS = 512
DRAFT_TOKENS = 4


epsilon = 1e-05


def as_sent(x):

    def short(part):
        return part.astype(jnp.bfloat16) if part.dtype == jnp.float32 else part

    return jax.tree.map(short, x)


def rotate(vectors, cos_table, sin_table):
    half_width = vectors.shape[-1] // 2
    first_half = vectors[..., :half_width]
    second_half = vectors[..., half_width:]
    return jnp.concatenate(
        [
            first_half * cos_table - second_half * sin_table,
            second_half * cos_table + first_half * sin_table,
        ],
        axis=-1,
    )


def rope_tables(positions):
    frequency = 10000.0 ** (-(jnp.arange(HEAD_SIZE // 2, dtype=jnp.float32) * 2.0 / HEAD_SIZE))
    angles = positions.astype(jnp.float32)[..., None] * frequency
    return (jnp.cos(angles), jnp.sin(angles))


def attend_one(queries, fresh_keys, fresh_values, key_tile_block, value_tile_block, length):
    score_scale = HEAD_SIZE ** (-0.5)
    scores_cache = (
        jnp.einsum("tkgd,pkd->kgtp", queries, key_tile_block, preferred_element_type=jnp.float32)
        * score_scale
    )
    scores_new = (
        jnp.einsum("tkgd,ukd->kgtu", queries, fresh_keys, preferred_element_type=jnp.float32)
        * score_scale
    )
    live_keys = jnp.arange(key_tile_block.shape[0], dtype=jnp.int32) < length
    causal = jnp.arange(DRAFT_TOKENS)[None, :] <= jnp.arange(DRAFT_TOKENS)[:, None]
    scores_cache = jnp.where(live_keys, scores_cache, -1e30)
    scores_new = jnp.where(causal, scores_new, -1e30)
    highest = jnp.maximum(jnp.max(scores_cache, axis=-1), jnp.max(scores_new, axis=-1))[..., None]
    weight_cache = jnp.exp(scores_cache - highest)
    weight_new = jnp.exp(scores_new - highest)
    denominator = jnp.sum(weight_cache, axis=-1, keepdims=True) + jnp.sum(
        weight_new, axis=-1, keepdims=True
    )
    probs_cache = (weight_cache / denominator).astype(jnp.bfloat16)
    probs_new = (weight_new / denominator).astype(jnp.bfloat16)
    attended = jnp.einsum(
        "kgtp,pkd->tkgd", probs_cache, value_tile_block, preferred_element_type=jnp.float32
    )
    attended = attended + jnp.einsum(
        "kgtu,ukd->tkgd", probs_new, fresh_values, preferred_element_type=jnp.float32
    )
    return attended.astype(jnp.bfloat16)


def scan_one(
    state_block, inputs_x, gates_z, b_vals, c_vals, step_sizes, decay_rates, skip_gain, head_gain
):
    hstate = state_block.astype(jnp.float32)
    in_active = jax.nn.silu(inputs_x.astype(jnp.float32))
    write_vec = jax.nn.silu(b_vals.astype(jnp.float32))
    read_vec = jax.nn.silu(c_vals.astype(jnp.float32))
    outputs = []
    for draft_index in range(DRAFT_TOKENS):
        decays = jnp.exp(-step_sizes[draft_index] * decay_rates)
        inject = (step_sizes[draft_index][:, None] * in_active[draft_index])[
            :, :, None
        ] * write_vec[draft_index][None, None, :]
        hstate = decays[:, None, None] * hstate + inject
        readout = jnp.einsum(
            "hpn,n->hp", hstate, read_vec[draft_index], precision=lax.Precision.HIGHEST
        )
        outputs.append(readout + skip_gain[:, None] * in_active[draft_index])
    gated = jnp.stack(outputs) * jax.nn.silu(gates_z.astype(jnp.float32))
    mean_square = jnp.mean(gated * gated, axis=-1, keepdims=True)
    return (gated * lax.rsqrt(mean_square + epsilon) * head_gain).astype(jnp.bfloat16)


def on_device(
    tokens,
    norm_gain,
    mixer_in,
    shared_in,
    step_in,
    step_bias,
    decay_rate,
    skip_gain,
    cached_keys,
    cached_values,
    lengths,
    state_cache,
    mixer_gain,
    mixer_out,
    gate_weight,
    up_weight,
    down_weight,
):
    short_count = lax.axis_size("short")
    n_wide = lax.axis_size("wide")
    q_heads = QUERY_HEADS // short_count
    key_value_heads = KEY_VALUE_HEADS // short_count
    ssm_heads = MH // short_count
    repeat_factor = QUERY_HEADS // KEY_VALUE_HEADS
    query_size = q_heads * HEAD_SIZE
    key_size = key_value_heads * HEAD_SIZE
    m_size = ssm_heads * MP
    local_rows = tokens.shape[0]
    requests = local_rows // DRAFT_TOKENS
    width_half = tokens.shape[1]
    rows_float = tokens.astype(jnp.float32)
    square_sum = lax.psum(jnp.sum(rows_float * rows_float, axis=1), "short")
    inv_rms = lax.rsqrt(square_sum / D + epsilon)
    normed = (rows_float * inv_rms[:, None] * norm_gain[None, :]).astype(jnp.bfloat16)
    step_terms = jnp.dot(normed, step_in, preferred_element_type=jnp.float32)
    step_raw = lax.psum_scatter(step_terms, "short", scatter_dimension=1, tiled=True)
    gathered = lax.all_gather(normed, "wide", axis=0, tiled=True)
    group_part = jnp.einsum("rd,dgc->rgc", gathered, mixer_in, preferred_element_type=jnp.float32)
    shared_part = jnp.dot(gathered, shared_in, preferred_element_type=jnp.float32)[:, None, :]
    gate_part = jnp.dot(gathered, gate_weight, preferred_element_type=jnp.float32)
    up_part = jnp.dot(gathered, up_weight, preferred_element_type=jnp.float32)
    gate_half, up_half = (
        lax.psum_scatter(
            gate_part.astype(jnp.bfloat16), "short", scatter_dimension=0, tiled=True
        ).astype(jnp.float32),
        lax.psum_scatter(
            up_part.astype(jnp.bfloat16), "short", scatter_dimension=0, tiled=True
        ).astype(jnp.float32),
    )
    hidden_half = (jax.nn.silu(gate_half) * up_half).astype(jnp.bfloat16)
    hidden = lax.all_gather(hidden_half, "short", axis=0, tiled=True)
    group_moved, shared_moved = (
        lax.all_to_all(group_part, "wide", split_axis=0, concat_axis=2, tiled=True),
        lax.all_to_all(shared_part, "wide", split_axis=0, concat_axis=2, tiled=True),
    )
    group_sum = lax.psum_scatter(group_moved, "short", scatter_dimension=1, tiled=True)
    shared_sum = lax.psum(shared_moved, "short")
    features = group_sum[:, 0, :].astype(jnp.bfloat16)
    shared_vals = shared_sum[:, 0, :].astype(jnp.bfloat16)
    queries = features[:, :query_size].reshape(requests, DRAFT_TOKENS, q_heads, HEAD_SIZE)
    fresh_keys = features[:, query_size : query_size + key_size].reshape(
        requests, DRAFT_TOKENS, key_value_heads, HEAD_SIZE
    )
    fresh_values = features[:, query_size + key_size : query_size + 2 * key_size].reshape(
        requests, DRAFT_TOKENS, key_value_heads, HEAD_SIZE
    )
    x_start = query_size + 2 * key_size
    inputs_x = features[:, x_start : x_start + m_size].reshape(
        requests, DRAFT_TOKENS, ssm_heads, MP
    )
    gates_z = features[:, x_start + m_size : x_start + 2 * m_size].reshape(
        requests, DRAFT_TOKENS, ssm_heads, MP
    )
    positions = lengths[:, None] + jnp.arange(DRAFT_TOKENS, dtype=jnp.int32)[None, :]
    cos_table, sin_table = rope_tables(positions)
    cos_table = cos_table[:, :, None, :]
    sin_table = sin_table[:, :, None, :]
    rotated_queries = rotate(queries.astype(jnp.float32), cos_table, sin_table).astype(jnp.bfloat16)
    keys_rot = rotate(fresh_keys.astype(jnp.float32), cos_table, sin_table).astype(jnp.bfloat16)
    rotated_queries = rotated_queries.reshape(
        requests, DRAFT_TOKENS, key_value_heads, repeat_factor, HEAD_SIZE
    )
    key_tile_block = cached_keys.reshape(requests, CACHE_SLOTS, key_value_heads, HEAD_SIZE)
    value_tile_block = cached_values.reshape(requests, CACHE_SLOTS, key_value_heads, HEAD_SIZE)
    attention = jax.vmap(attend_one)(
        rotated_queries, keys_rot, fresh_values, key_tile_block, value_tile_block, lengths
    )
    step_sizes = jax.nn.softplus(
        step_raw.reshape(requests, DRAFT_TOKENS, ssm_heads) + step_bias[None, None, :]
    )
    b_vals = shared_vals[:, :NS].reshape(requests, DRAFT_TOKENS, NS)
    c_vals = shared_vals[:, NS:].reshape(requests, DRAFT_TOKENS, NS)
    head_gain = mixer_gain.reshape(ssm_heads, MP)
    mamba = jax.vmap(scan_one, in_axes=(0, 0, 0, 0, 0, 0, None, None, None))(
        state_cache, inputs_x, gates_z, b_vals, c_vals, step_sizes, decay_rate, skip_gain, head_gain
    )
    own_rows = jnp.concatenate(
        [attention.reshape(local_rows, query_size), mamba.reshape(local_rows, m_size)], axis=1
    )
    returned = lax.all_to_all(
        as_sent(own_rows[:, None, :]), "wide", split_axis=2, concat_axis=0, tiled=True
    )
    both_groups = lax.all_gather(as_sent(returned), "short", axis=1, tiled=True).astype(
        returned.dtype
    )
    projected = jnp.einsum(
        "rgc,gcd->rd", both_groups, mixer_out, preferred_element_type=jnp.float32
    )
    summed = projected + jnp.dot(hidden, down_weight, preferred_element_type=jnp.float32)
    pieces = lax.all_to_all(
        summed.reshape(n_wide, local_rows, width_half).astype(jnp.bfloat16),
        "wide",
        split_axis=0,
        concat_axis=0,
        tiled=True,
    ).astype(jnp.float32)
    total = rows_float + jnp.sum(pieces, axis=0)
    return total.astype(jnp.bfloat16)


MESH = pl.DeviceIdType.MESH
F32 = jnp.float32
BF16 = jnp.bfloat16
NT = (((1,), (1,)), ((), ()))
LANE = 128


def silu(v):
    return v / (1.0 + jnp.exp(-v))


def dot(a, b):
    return jnp.dot(a, b, preferred_element_type=F32)


def dot_nt(a, b):
    return lax.dot_general(a, b, NT, preferred_element_type=F32)


def rope_rows(length, rows):
    lane = lax.broadcasted_iota(jnp.int32, (rows, HEAD_SIZE), 1)
    token = lax.broadcasted_iota(jnp.int32, (rows, HEAD_SIZE), 0)
    pair = lax.rem(lane, HEAD_SIZE // 2).astype(F32)
    angle = (token + length).astype(F32) * jnp.exp(pair * (-2.0 * math.log(10000.0) / HEAD_SIZE))
    turns = jnp.floor(angle * (2.0 / math.pi) + 0.5)
    rest = angle - turns * 1.5703125
    rest = rest - turns * 4.837512969970703125e-4
    rest = rest - turns * 7.54978995489188216e-8
    z = rest * rest
    sine = ((-1.9515295891e-4 * z + 8.3321608736e-3) * z - 1.6666654611e-1) * z * rest + rest
    cosine = (2.443315711809948e-5 * z - 1.388731625493765e-3) * z + 4.166664568298827e-2
    cosine = cosine * z * z - 0.5 * z + 1.0
    quarter = turns - 4.0 * jnp.floor(turns * 0.25)
    odd = (quarter == 1.0) | (quarter == 3.0)
    cos_t = jnp.where(odd, sine, cosine)
    cos_t = jnp.where((quarter == 1.0) | (quarter == 2.0), -cos_t, cos_t)
    sin_t = jnp.where(odd, cosine, sine)
    sin_t = jnp.where(quarter >= 2.0, -sin_t, sin_t)
    return cos_t, jnp.where(lane < HEAD_SIZE // 2, -sin_t, sin_t)


def fused_kernel(
    dims,
    tokens, gain_h, bias_h, rate_h, skip_h, lengths, mixer_gain_h,
    mixer_in, shared_in, step_in, keys, values, state, mixer_out, gate, up, down,
    out,
    gain, bias, rate, skip, mixer_gain,
    w_a, w_b, k_v, v_v, s_v, g_v, u_v, m_v, d_v,
    xg, xf, xb, p_send, p_recv, c_b, tot, step_f,
    f_send, f_recv, feat, bc, qbuf, knbuf, vnbuf, obuf, cbuf, rbuf, own,
    m_send, m_recv, lhs, lhs_b, gsc, gu_send, gu_recv, gl_send, gl_recv, hbuf, o_send, o_recv,
    sem_w, sem_loc, sem_r, sem_gs, sem_gr, sem_ps, sem_pr, sem_fs, sem_fr,
    sem_ms, sem_mr, sem_us, sem_ur, sem_hs, sem_hr, sem_os, sem_or,
):
    n, n_short, rows, width, gcol, scol, ncol, ocol, fspans, ospans = dims
    n_chunk = len(fspans)
    n_oc = len(ospans)
    total_rows = n * rows
    me = lax.axis_index("wide")
    s = lax.axis_index("short")
    other = 1 - s
    q_heads = QUERY_HEADS // n_short
    kv_heads = KEY_VALUE_HEADS // n_short
    m_heads = MH // n_short
    rep = QUERY_HEADS // KEY_VALUE_HEADS
    acol = gcol + scol + ncol
    sq_width = round_up(acol + 1) - acol
    fpad = xpad(gcol)
    opad = round_up(ocol + ocol % LANE)

    def peer(d):
        return lax.rem(me + d, n)

    def upward(k):
        return jnp.where(me <= k, k + 1, k)

    def far_first(k):
        down_to = n - 1 - k
        return jnp.where(2 * me >= n, upward(k), jnp.where(down_to > me, down_to, down_to - 1))

    weights = []

    def fetch(src, dst):
        copy = pltpu.make_async_copy(src, dst, sem_w.at[len(weights)])
        copy.start()
        weights.append(copy)
        return copy

    late = n // 2
    early = me < late

    def tell(sem, wide, short):
        pl.semaphore_signal(
            sem, inc=1, device_id={"wide": wide, "short": short}, device_id_type=MESH
        )

    barrier = pltpu.get_barrier_semaphore()
    for k in range(late):
        to = n - 1 - k

        @pl.when((me != to) if to >= n - 2 else (me != to) & (me != 2 * n - 5 - to))
        def _(to=to):
            tell(barrier, to, s)

    @pl.when(early)
    def _():
        for k in range(1, late):
            tell(barrier, lax.rem(me + k, late), s)

    tell(barrier, me, other)

    own_tokens = fetch(tokens, xg.at[me])
    small = [
        fetch(gain_h, gain), fetch(bias_h, bias), fetch(rate_h, rate), fetch(skip_h, skip),
        fetch(mixer_gain_h, mixer_gain),
    ]
    lead = dims_lead(gcol)
    sem_a = len(weights)
    for src, dst in (
        (mixer_in.at[s, pl.ds(0, lead)], w_a.at[pl.ds(0, lead)]),
        (mixer_in.at[other], w_a.at[pl.ds(lead, gcol)]),
        (shared_in, w_a.at[pl.ds(lead + gcol, scol)]),
        (step_in, w_a.at[pl.ds(lead + gcol + scol, ncol)]),
    ):
        pltpu.make_async_copy(src, dst, sem_w.at[sem_a]).start()
    weights.append(None)
    fb = [fetch(mixer_in.at[s, pl.ds(lead, gcol - lead)], w_b)]

    def cols(c):
        return pl.ds(*fspans[c])

    fgu = []
    for c in range(n_chunk):
        fgu.append(
            (fetch(gate.at[:, cols(c)], g_v.at[:, cols(c)]), fetch(up.at[:, cols(c)], u_v.at[:, cols(c)]))
        )
        if c == 0:
            fkv = [fetch(keys, k_v), fetch(values, v_v), fetch(state, s_v)]
    fdn = [fetch(down.at[cols(c)], d_v.at[cols(c)]) for c in range(n_chunk)]
    sem_m = len(weights)
    for g in range(n_short):
        pltpu.make_async_copy(
            mixer_out.at[g], m_v.at[pl.ds(g * ocol, ocol)], sem_w.at[sem_m]
        ).start()

    def remote(src, dst, send, recv, wide, short):
        copy = pltpu.make_async_remote_copy(
            src_ref=src, dst_ref=dst, send_sem=send, recv_sem=recv,
            device_id={"wide": wide, "short": short}, device_id_type=MESH,
        )
        copy.start()
        return copy

    def arrived(buf, recv):
        pltpu.make_async_copy(buf, buf, recv).wait()

    sent = []

    def give(wide):
        remote(xg.at[me], xg.at[me], sem_gs, sem_gr, wide, s)

    pl.semaphore_wait(barrier, jnp.where(early, late, jnp.where(me < n - 2, n - 1, n)))
    own_tokens.wait()
    side = lax.rem(me, 2)
    beside = me + 1 - 2 * side

    @pl.when(early)
    def _():
        for k in range(1, late):
            give(lax.rem(me + k, late))
        pl.semaphore_wait(sem_r.at[0], 1)
        give(n - 2 + side)
        give(n - 3 - side)
        give(n - 4 + side)
        pl.semaphore_wait(sem_r.at[1], 1)
        give(n - 1 - side)

    @pl.when((me >= late) & (me < n - 2))
    def _():
        tell(sem_r.at[0], me - 2, s)
        tell(sem_r.at[0], me - 4, s)
        tell(sem_r.at[1], beside - 2, s)
        tell(sem_r.at[1], beside - 4, s)
        tell(sem_r.at[0], beside, s)
        for k in range(late):
            give(k)
        give(beside)
        give(n - 2 + side)
        pl.semaphore_wait(sem_r.at[0], 1)
        give(n - 1 - side)

    @pl.when(me >= n - 2)
    def _():
        for k in range(n - 2):
            give(k)
        give(beside)

    feat[...] = jnp.zeros_like(feat)
    bc[...] = jnp.zeros_like(bc)
    qbuf[...] = jnp.zeros_like(qbuf)
    knbuf[...] = jnp.zeros_like(knbuf)
    vnbuf[...] = jnp.zeros_like(vnbuf)
    cbuf[...] = jnp.zeros_like(cbuf)
    c_b[...] = jnp.zeros_like(c_b)
    tot[...] = jnp.zeros_like(tot)
    own[...] = jnp.zeros_like(own)
    for copy in small:
        copy.wait()
    cos_t, sin_t = rope_rows(lengths[0], rows)
    arrived(xg.at[pl.ds(0, n - 1)], sem_gr)
    for j in range(n):
        xf[rows * j : rows * (j + 1), :] = xg[j].astype(F32)
    x = xf[...]
    squares = jnp.sum(x * x, axis=1, keepdims=True)
    p_send[:, acol:] = jnp.broadcast_to(squares, (total_rows, sq_width))
    for j in range(width // LANE):
        lanes = slice(j * LANE, (j + 1) * LANE)
        xb[:, lanes] = (xf[:, lanes] * gain[j : j + 1, :]).astype(BF16)

    arrived(w_a, sem_w.at[sem_a])
    both = dot_nt(xb[...], w_a[...])
    p_send[:, :acol] = both[:, lead:]
    c_b[:, :lead] = both[:, :lead]
    sent.append(remote(p_send, p_recv, sem_ps, sem_pr, me, other))
    fb[0].wait()
    c_b[:, lead:gcol] = dot_nt(xb[...], w_b[...])
    lane = lax.broadcasted_iota(jnp.int32, (total_rows, acol), 1)
    mine = jnp.where(lane < gcol, c_b[:, :acol], p_send[:, :acol])
    arrived(p_recv, sem_pr)
    mean_square = (squares + p_recv[:, acol : acol + 1]) / D
    inv = lax.rsqrt(mean_square + epsilon)
    tot[:, :acol] = (mine + p_recv[:, :acol]) * inv
    whole = tot[...]
    wide_lane = lax.broadcasted_iota(jnp.int32, whole.shape, 1)
    span = whole.shape[1]
    features = pltpu.roll(
        jnp.where(wide_lane < gcol, whole, 0.0), lax.rem(me * gcol, LANE), 1
    )
    low = pltpu.roll(whole, span - scol - gcol, 1)
    step_all = pltpu.roll(whole, span - gcol - scol, 1)[:, :LANE]
    step_f[...] = pltpu.roll(step_all, lax.rem(LANE - s * m_heads, LANE), 1)
    tot[...] = jnp.where(wide_lane < span - scol, features, low)
    for r in range(n):
        f_send[r] = tot[rows * r : rows * (r + 1), :].astype(BF16)
    for k in range(n - 1):
        to = far_first(k)
        remote(f_send.at[to], f_recv.at[me], sem_fs, sem_fr, to, s)
    own_f = pltpu.make_async_copy(f_send.at[me], f_recv.at[me], sem_loc.at[0])
    own_f.start()

    half = total_rows // n_short

    def gate_up(c):
        part = slice(fspans[c][0], fspans[c][0] + fspans[c][1])
        fgu[c][0].wait()
        fgu[c][1].wait()
        both = [dot(xb[...], g_v[:, part]), dot(xb[...], u_v[:, part])]
        for k in range(2):
            for i in range(n_short):
                gsc[k, i, :, part] = both[k][half * i : half * (i + 1)] * inv[half * i : half * (i + 1)]
        if c:
            late_cols = pl.ds(fspans[c][0] - fspans[0][1], fspans[c][1])
            for k in range(2):
                gl_send[k, :, late_cols] = (both[k] * inv).astype(BF16)
            sent.append(
                remote(
                    gl_send.at[:, :, late_cols], gl_recv.at[:, :, late_cols],
                    sem_us.at[c], sem_ur.at[c], me, other,
                )
            )
            return
        for k in range(2):
            gu_send[k, :, part] = gsc[k, other, :, part].astype(BF16)
        sent.append(
            remote(
                gu_send.at[:, :, cols(c)], gu_recv.at[:, :, cols(c)], sem_us.at[c], sem_ur.at[c], me, other
            )
        )

    def hidden(c):
        part = slice(fspans[c][0], fspans[c][0] + fspans[c][1])
        if c:
            late_cols = pl.ds(fspans[c][0] - fspans[0][1], fspans[c][1])
            arrived(gl_recv.at[:, :, late_cols], sem_ur.at[c])
            for i in range(n_short):
                here = slice(half * i, half * (i + 1))
                a = gsc[0, i, :, part] + gl_recv[0, here, late_cols].astype(F32)
                b = gsc[1, i, :, part] + gl_recv[1, here, late_cols].astype(F32)
                hbuf[i, :, part] = (silu(a) * b).astype(BF16)
            return
        arrived(gu_recv.at[:, :, cols(c)], sem_ur.at[c])
        a = gsc[0, s, :, part] + gu_recv[0, :, part].astype(F32)
        b = gsc[1, s, :, part] + gu_recv[1, :, part].astype(F32)
        hbuf[s, :, part] = (silu(a) * b).astype(BF16)
        sent.append(
            remote(
                hbuf.at[s, :, cols(c)], hbuf.at[s, :, cols(c)], sem_hs.at[c], sem_hr.at[c], me, other
            )
        )

    def down_part(at, size):
        part = slice(at, at + size)
        term = dot(hbuf[:, :, part].reshape(total_rows, size), d_v[part, :])
        xf[...] = term if at == 0 else xf[...] + term

    def hidden_in(c):
        if c == 0:
            arrived(hbuf.at[other, :, cols(c)], sem_hr.at[c])
        fdn[c].wait()

    gate_up(0)

    own_f.wait()
    arrived(f_recv.at[pl.ds(0, n - 1)], sem_fr)
    fwidth = feat.shape[1]
    tail_lane = lax.broadcasted_iota(jnp.int32, (rows, LANE), 1)
    for j in range(n):
        base = gcol * j // LANE * LANE
        w = min(fpad, fwidth - base)
        block = f_recv[j].astype(F32)
        tail = block[:, fpad - LANE :]
        block = jnp.concatenate(
            [block[:, : fpad - LANE], jnp.where(tail_lane < LANE - scol, tail, 0.0)], axis=1
        )
        feat[:, base : base + w] += block[:, :w]
        base = scol * j // LANE * LANE
        tail = jnp.where(tail_lane < LANE - scol, 0.0, tail)
        move = (scol * (j + 1)) % LANE
        bc[:, base : base + LANE] += pltpu.roll(tail, move, 1) if move else tail
    for copy in fkv:
        copy.wait()
    k_at = q_heads * HEAD_SIZE
    v_at = k_at + kv_heads * HEAD_SIZE
    x_at = v_at + kv_heads * HEAD_SIZE
    z_at = x_at + m_heads * MP

    def turn(v):
        return v * cos_t + jnp.concatenate([v[:, HEAD_SIZE // 2 :], v[:, : HEAD_SIZE // 2]], axis=1) * sin_t

    length = lengths[0]
    for kv in range(kv_heads):
        for i in range(rep):
            h = kv * rep + i
            qbuf[kv, rows * i : rows * (i + 1), :] = turn(feat[:, h * HEAD_SIZE : (h + 1) * HEAD_SIZE])
        knbuf[kv, :rows, :] = turn(feat[:, k_at + kv * HEAD_SIZE : k_at + (kv + 1) * HEAD_SIZE])
        vnbuf[kv, :rows, :] = feat[:, v_at + kv * HEAD_SIZE : v_at + (kv + 1) * HEAD_SIZE]
        head = slice(kv * HEAD_SIZE, (kv + 1) * HEAD_SIZE)
        query = qbuf[kv].astype(BF16)
        scale = HEAD_SIZE ** (-0.5)
        old = dot_nt(query, k_v[:, head]) * scale
        new = dot_nt(query, knbuf[kv].astype(BF16)) * scale
        slot = lax.broadcasted_iota(jnp.int32, old.shape, 1)
        old = jnp.where(slot < length, old, -1e30)
        token = lax.rem(lax.broadcasted_iota(jnp.int32, new.shape, 0), rows)
        fresh = lax.broadcasted_iota(jnp.int32, new.shape, 1)
        new = jnp.where(fresh <= token, new, -1e30)
        top = jnp.maximum(
            jnp.max(old, axis=1, keepdims=True), jnp.max(new, axis=1, keepdims=True)
        )
        old = jnp.exp(old - top)
        new = jnp.exp(new - top)
        den = jnp.sum(old, axis=1, keepdims=True) + jnp.sum(new, axis=1, keepdims=True)
        obuf[kv] = (
            dot(old.astype(BF16), v_v[:, head]) + dot(new.astype(BF16), vnbuf[kv].astype(BF16))
        ) / den
        for i in range(rep):
            h = kv * rep + i
            own[:, h * HEAD_SIZE : (h + 1) * HEAD_SIZE] = obuf[kv, rows * i : rows * (i + 1), :]

    write = silu(bc[:, :NS])
    read = silu(bc[:, NS:])
    rest = read
    for i in range(3):
        piece = rest.astype(BF16).astype(F32)
        cbuf[rows * i : rows * (i + 1), :] = piece
        rest = rest - piece
    rbuf[...] = dot_nt(cbuf[...].astype(BF16), s_v[...])
    carried = rbuf[:rows] + rbuf[rows : 2 * rows] + rbuf[2 * rows : 3 * rows]
    raw = step_f[pl.ds(rows * me, rows), :][:, :m_heads] + bias[...]
    step = jnp.maximum(raw, 0.0) + jnp.log1p(jnp.exp(-jnp.abs(raw)))
    run = [step[:1]]
    for t in range(1, rows):
        run.append(run[-1] + step[t : t + 1])
    age = jnp.concatenate(run, axis=0) * rate[...]
    kept = jnp.exp(-age)
    tid = lax.broadcasted_iota(jnp.int32, age.shape, 0)
    mix = []
    for u in range(rows):
        overlap = jnp.sum(read * write[u : u + 1], axis=1, keepdims=True)
        fade = jnp.exp(-jnp.maximum(age - age[u : u + 1], 0.0))
        mix.append(jnp.where(tid >= u, fade, 0.0) * step[u : u + 1] * overlap)
    skips = skip[...]
    for h in range(m_heads):
        hs = slice(h * MP, (h + 1) * MP)
        active = silu(feat[:, x_at + h * MP : x_at + (h + 1) * MP])
        y = kept[:, h : h + 1] * carried[:, hs] + skips[:, h : h + 1] * active
        for u in range(rows):
            y = y + mix[u][:, h : h + 1] * active[u : u + 1]
        y = y * silu(feat[:, z_at + h * MP : z_at + (h + 1) * MP])
        ms = jnp.mean(y * y, axis=1, keepdims=True)
        at = (q_heads + h) * MP
        own[:, at : at + MP] = y * lax.rsqrt(ms + epsilon) * mixer_gain[:, hs]

    window = opad + LANE
    for j in range(n):
        base = ocol * j // LANE * LANE
        off = ocol * j - base
        v = own[:, base : base + window]
        if off:
            v = jnp.concatenate([v[:, off:], v[:, :off]], axis=1)
        m_send[j] = v[:, :opad].astype(BF16)
    for k in range(n):
        to = far_first(k) if k < n - 1 else me
        for e in range(n_short):
            if k < n - 1 or e:
                remote(
                    m_send.at[to], m_recv.at[s * n + me], sem_ms, sem_mr, to, lax.rem(s + e, n_short)
                )
    own_m = pltpu.make_async_copy(m_send.at[me], m_recv.at[s * n + me], sem_loc.at[1])
    own_m.start()

    hidden(0)
    for c in range(1, n_chunk):
        gate_up(c)
    hidden_in(0)
    pieces = spans_of(fspans[0][1], 1024)
    for k, (at, size) in enumerate(pieces):
        if k == len(pieces) - 1:
            for c in range(1, n_chunk):
                hidden(c)
        down_part(at, size)
    for c in range(1, n_chunk):
        hidden_in(c)
        down_part(*fspans[c])
    own_m.wait()
    arrived(m_recv.at[pl.ds(0, n * n_short - 1)], sem_mr)
    for g in range(n_short):
        for j in range(n):
            lhs[g, rows * j : rows * (j + 1), :] = m_recv[g * n + j].astype(F32)
    shift = ocol % LANE
    at = ocol - shift
    block_lane = lax.broadcasted_iota(jnp.int32, (total_rows, opad), 1)
    first = jnp.where(block_lane < ocol, lhs[0], 0.0)
    second = pltpu.roll(lhs[1], shift, 1) if shift else lhs[1]
    second = jnp.where((block_lane >= shift) & (block_lane < shift + ocol), second, 0.0)
    lhs_b[:, :at] = first[:, :at].astype(BF16)
    lhs_b[:, at:opad] = (first[:, at:] + second[:, : opad - at]).astype(BF16)
    lhs_b[:, opad:] = second[:, opad - at :].astype(BF16)
    arrived(m_v, sem_w.at[sem_m])
    def out_to(o, k):
        to = upward(k)
        part = pl.ds(*ospans[o])
        remote(o_send.at[to, :, part], o_recv.at[me, :, part], sem_os.at[o], sem_or.at[o], to, s)

    for o in range(n_oc):
        oc = slice(ospans[o][0], ospans[o][0] + ospans[o][1])
        acc = xf[:, oc] + dot(lhs_b[:, : n_short * ocol], m_v[:, oc])
        xf[:, oc] = acc
        for r in range(n):
            o_send[r, :, oc] = xf[rows * r : rows * (r + 1), oc].astype(BF16)
        out_to(o, 0)
        if o:
            for k in range(1, n - 1):
                out_to(o - 1, k)
    for k in range(1, n - 1):
        out_to(n_oc - 1, k)
    for o in range(n_oc):
        part = pl.ds(*ospans[o])
        oc = slice(ospans[o][0], ospans[o][0] + ospans[o][1])
        acc = xg[me, :, oc].astype(F32) + o_send[me, :, oc].astype(F32)
        arrived(o_recv.at[pl.ds(0, n - 1), :, part], sem_or.at[o])
        for d in range(1, n):
            acc = acc + o_recv[peer(d), :, oc].astype(F32)
        out[:, oc] = acc.astype(BF16)
    for copy in sent:
        copy.wait_send()
    arrived(xg.at[pl.ds(0, n - 1)], sem_gs)
    arrived(f_send.at[pl.ds(0, n - 1)], sem_fs)
    arrived(m_recv.at[pl.ds(0, n * n_short - 1)], sem_ms)
    for o in range(n_oc):
        arrived(o_send.at[pl.ds(0, n - 1), :, pl.ds(*ospans[o])], sem_os.at[o])


def round_up(v):
    return -(-v // LANE) * LANE


def dims_lead(gcol):
    return min(LANE, gcol - 16)


def xpad(gcol):
    return round_up(gcol + LANE - 1)


def spans_of(width, piece):
    return tuple((at, min(piece, width - at)) for at in range(0, width, piece))


def fused(*args):
    (tokens, norm_gain, mixer_in, shared_in, step_in, step_bias, decay_rate, skip_gain,
     cached_keys, cached_values, lengths, state_cache, mixer_gain, mixer_out,
     gate_weight, up_weight, down_weight) = args
    n = lax.axis_size("wide")
    n_short = lax.axis_size("short")
    rows, width = tokens.shape
    gcol = mixer_in.shape[2]
    scol = shared_in.shape[1]
    ncol = step_in.shape[1]
    ocol = mixer_out.shape[1]
    ffl = gate_weight.shape[1]
    fspans = spans_of(ffl, 2048)
    first = min(1024, width)
    ospans = ((0, first),) + tuple((first + at, size) for at, size in spans_of(width - first, 1536))
    n_chunk = len(fspans)
    n_oc = len(ospans)
    m_heads = MH // n_short
    kv_heads = KEY_VALUE_HEADS // n_short
    remain = max(LANE, ffl - fspans[0][1])
    total_rows = n * rows
    acol = gcol + scol + ncol
    sq_width = round_up(acol + 1) - acol
    fpad = xpad(gcol)
    opad = round_up(ocol + ocol % LANE)
    lead = dims_lead(gcol)
    features = n * gcol
    outs = n * ocol
    half = total_rows // n_short
    dims = (n, n_short, rows, width, gcol, scol, ncol, ocol, fspans, ospans)
    vm = pl.BlockSpec(memory_space=pltpu.VMEM)
    hb = pl.BlockSpec(memory_space=pl.ANY)
    V = pltpu.VMEM
    dma = pltpu.SemaphoreType.DMA
    kvw = cached_keys.shape[2]
    slots = cached_keys.shape[1]
    scratch = [
        V((width // LANE, LANE), F32), V((1, m_heads), F32), V((1, m_heads), F32),
        V((1, m_heads), F32), V((1, m_heads * MP), F32),
        V((lead + acol, width), BF16), V((gcol - lead, width), BF16), V((slots, kvw), BF16),
        V((slots, kvw), BF16), V((m_heads * MP, NS), BF16),
        V((width, ffl), BF16), V((width, ffl), BF16),
        V((n_short * ocol, width), BF16), V((ffl, width), BF16),
        V((n, rows, width), BF16), V((total_rows, width), F32), V((total_rows, width), BF16),
        V((total_rows, acol + sq_width), F32), V((total_rows, acol + sq_width), F32),
        V((total_rows, fpad), F32),
        V((total_rows, fpad), F32), V((total_rows, LANE), F32),
        V((n, rows, fpad), BF16), V((n, rows, fpad), BF16),
        V((rows, features), F32), V((rows, 2 * NS), F32),
        V((kv_heads, 32, HEAD_SIZE), F32), V((kv_heads, 16, HEAD_SIZE), F32),
        V((kv_heads, 16, HEAD_SIZE), F32), V((kv_heads, 32, HEAD_SIZE), F32),
        V((16, NS), F32), V((16, m_heads * MP), F32),
        V((rows, round_up(outs) + opad + LANE), F32),
        V((n, rows, opad), BF16), V((n_short * n, rows, opad), BF16),
        V((n_short, total_rows, opad), F32), V((total_rows, ocol // LANE * LANE + opad), BF16),
        V((2, n_short, half, ffl), F32),
        V((2, half, ffl), BF16), V((2, half, ffl), BF16),
        V((2, total_rows, remain), BF16), V((2, total_rows, remain), BF16),
        V((n_short, half, ffl), BF16),
        V((n, rows, width), BF16), V((n, rows, width), BF16),
        dma((6 + 2 + 3 * n_chunk + 3 + 1,)), dma((2,)),
        pltpu.SemaphoreType.REGULAR((2,)), dma, dma, dma, dma, dma, dma,
        dma, dma, dma((n_chunk,)), dma((n_chunk,)),
        dma((1,)), dma((1,)), dma((n_oc,)), dma((n_oc,)),
    ]
    return pl.pallas_call(
        functools.partial(fused_kernel, dims),
        out_shape=pltpu.VMEM((rows, width), BF16),
        in_specs=[hb] * 5 + [pl.BlockSpec(memory_space=pltpu.SMEM)] + [hb] * 11,
        out_specs=vm,
        scratch_shapes=scratch,
        name="layer",
        compiler_params=pltpu.CompilerParams(
            collective_id=0, has_side_effects=True, vmem_limit_bytes=66 * 1000 * 1000
        ),
    )(
        tokens, norm_gain.reshape(width // LANE, LANE), step_bias[None, :], decay_rate[None, :],
        skip_gain[None, :], lengths, mixer_gain[None, :],
        jnp.transpose(mixer_in, (1, 2, 0)), shared_in.T, step_in.T,
        cached_keys[0], cached_values[0], state_cache.reshape(m_heads * MP, NS),
        mixer_out, gate_weight, up_weight, down_weight,
    )


def roomy(n, gcol, scol):
    return max(gcol * j % LANE for j in range(n)) + gcol <= xpad(gcol) - scol


def fits(n, n_short, args):
    tokens, mixer_in, shared_in, step_in = args[0], args[2], args[3], args[4]
    return (
        n_short == 2
        and tokens.shape[0] == DRAFT_TOKENS
        and n * DRAFT_TOKENS == 32
        and mixer_in.shape[2] % 16 == 0
        and shared_in.shape[1] % 16 == 0
        and LANE % shared_in.shape[1] == 0
        and shared_in.shape[1] < LANE
        and roomy(n, mixer_in.shape[2], shared_in.shape[1])
        and step_in.shape[1] % 16 == 0
        and args[13].shape[1] % 16 == 0
        and args[13].shape[1] >= LANE
        and args[14].shape[1] % LANE == 0
        and tokens.shape[1] % LANE == 0
    )


def layer(*args):
    if fits(lax.axis_size("wide"), lax.axis_size("short"), args):
        return fused(*args)
    return on_device(*args)


def solution(mesh):
    in_specs = (
        P(("groups", "wide"), "short"),
        P("short"),
        P("short", None, "wide"),
        P("short", "wide"),
        P("short", None),
        P("short"),
        P("short"),
        P("short"),
        P(("groups", "wide"), None, "short"),
        P(("groups", "wide"), None, "short"),
        P(("groups", "wide")),
        P(("groups", "wide"), "short", None, None),
        P("short"),
        P(None, "wide", "short"),
        P("short", "wide"),
        P("short", "wide"),
        P("wide", "short"),
    )
    out_specs = P(("groups", "wide"), "short")
    return jax.shard_map(
        layer, mesh=mesh, in_specs=in_specs, out_specs=out_specs, check_vma=False
    )
```
